128 devices in a mesh: row: 4 (over y), col: 8 (over x, core), seq: 4 (over z).
Axes of the slice: x: 4, y: 4, z: 4, core: 2. Of those that a mesh axis runs over, the one named last changes fastest.
Arguments:
- hidden_in: bfloat16 [4, 48, 8192], P(None, None, 'row'), may hold values from -80 to 80, as said below
- norm_gain: bfloat16 [8192], replicated, may hold values from 0.099609375 to 1.8984375
- w_qkv: bfloat16 [8192, 10240], P('row', 'col'), may hold values from -0.0625 to 0.0625
- w_out: bfloat16 [8192, 8192], P('col', 'row'), may hold values from -0.0625 to 0.0625
- kv_pool: bfloat16 [4096, 2, 64, 1024], P(('row', 'seq'), None, None, 'col'), may hold values from -70 to 70, as said below
- page_owner: int32 [4096], replicated, may hold values from -1 to 51, as said below
- page_fill: int32 [4096], replicated, may hold values from 0 to 64, as said below
- lengths: int32 [48], replicated, may hold values from 65 to 16896, as said below
- group_of_request: int32 [48], replicated, may hold values from 0 to 3, as said below
- migrate_dest: int32 [4096], replicated, may hold values from 0 to 15, as said below
Outputs:
- layer_out: bfloat16 [4, 48, 8192], P(None, 'seq', ('row', 'col'))
- new_kv: bfloat16 [4, 48, 2, 1024], P(None, 'seq', None, 'col')
- new_pool: bfloat16 [4096, 2, 64, 1024], P(('row', 'seq'), None, None, 'col')
The draws below stay inside these ranges and needn't reach their ends.
Inputs may be any that keep to these rules, and one draw needn't show every extreme that they name: `hidden_in`: drawn values. `kv_pool`: drawn values. `page_owner`: A shared prompt of a group owns up to 256 pages and a request up to 8 own pages; a page's valid tokens lead, only the last page of an owner is partly filled; within each block of 256 slots the non-empty slots come first, at most 128 of them, and some block holds exactly that many. `page_fill`: 0 exactly for empty slots. `lengths`: equals the valid tokens of the request's pages and of its group's prompt pages. `group_of_request`: each group has 1 to 16 requests, some group exactly 16. `migrate_dest`: each block of 256 slots names every destination exactly 16 times.
All inputs are finite; a program needn't handle non-finite values.
Results may differ from the reference program's by a relative error of at most 0.02.
Values may be sent and summed in bfloat16 or wider, within the bound.
No kernel may reach another device: no remote copies, remote signals or barrier semaphores. Data moves between devices by JAX's collectives and lax.ppermute only.
A program may use at most 192 MiB of HBM per device.

```python
import jax
import jax.numpy as jnp
from jax import lax

D = 8192
HEADS = 64
KV_HEADS = 8
HEAD = 128
REQ = 48
GROUPS = 4
MEM = 16
STEPS = 4
PAGE = 64
POOL_DEV = 256
SPLITS = 16
NPAGES = 4096
CAP = 16
PROMPT_PAGES = 256
OWN_PAGES = 8
QKV_COLS = 10240


def layout(key):
    subkeys = jax.random.split(jax.random.fold_in(key, 11), 7)
    spare = (GROUPS - 1) * (MEM - 1)
    extra = REQ - MEM - (GROUPS - 1)
    chosen = (jax.random.permutation(subkeys[0], spare) < extra).astype(jnp.int32)
    sizes_rest = 1 + chosen.reshape(GROUPS - 1, MEM - 1).sum(1)
    sizes = jnp.concatenate([jnp.array([MEM], jnp.int32), sizes_rest])
    largest = jax.random.randint(subkeys[1], (), 0, GROUPS)
    sizes = jnp.roll(sizes, largest)
    bounds = jnp.cumsum(sizes)
    order = jax.random.permutation(subkeys[2], REQ)
    position_group = jnp.sum(jnp.arange(REQ)[:, None] >= bounds[None, :], 1).astype(jnp.int32)
    group = jnp.zeros((REQ,), jnp.int32).at[order].set(position_group)
    prompt_len = jax.random.randint(subkeys[3], (GROUPS,), PAGE, PROMPT_PAGES * PAGE + 1)
    prompt_len = prompt_len.at[largest].set(PROMPT_PAGES * PAGE)
    own_len = jax.random.randint(subkeys[4], (REQ,), 1, OWN_PAGES * PAGE + 1)
    first_member = jnp.argmax((group == largest).astype(jnp.int32))
    own_len = own_len.at[first_member].set(OWN_PAGES * PAGE)
    lengths = prompt_len[group] + own_len
    prompt_index = jnp.arange(PROMPT_PAGES)[None, :] * PAGE
    own_index = jnp.arange(OWN_PAGES)[None, :] * PAGE
    live = jnp.concatenate([(prompt_index < prompt_len[:, None]).reshape(-1), (own_index < own_len[:, None]).reshape(-1)])
    fill = jnp.concatenate([jnp.clip(prompt_len[:, None] - prompt_index, 0, PAGE).reshape(-1), jnp.clip(own_len[:, None] - own_index, 0, PAGE).reshape(-1)])
    owner = jnp.concatenate([jnp.broadcast_to(REQ + jnp.arange(GROUPS)[:, None], (GROUPS, PROMPT_PAGES)).reshape(-1), jnp.broadcast_to(jnp.arange(REQ)[:, None], (REQ, OWN_PAGES)).reshape(-1)])
    listed = GROUPS * PROMPT_PAGES + REQ * OWN_PAGES
    score = jnp.where(live, jax.random.permutation(subkeys[5], listed), listed + jnp.arange(listed))
    index = jnp.argsort(score)
    live_sorted = live[index]
    fill_sorted = fill[index]
    owner_sorted = owner[index]
    counter = jnp.arange(listed)
    half_pool = POOL_DEV // 2
    holders = jax.random.permutation(subkeys[6], SPLITS)
    slot = holders[jnp.clip(counter // half_pool, 0, SPLITS - 1)] * POOL_DEV + counter % half_pool
    target = jnp.where(live_sorted, slot, NPAGES)
    owner_all = jnp.full((NPAGES,), -1, jnp.int32).at[target].set(owner_sorted.astype(jnp.int32), mode='drop')
    fill_all = jnp.zeros((NPAGES,), jnp.int32).at[target].set(fill_sorted.astype(jnp.int32), mode='drop')
    return (owner_all, fill_all, lengths.astype(jnp.int32), group)


def draw_page_owner(key, part):
    return layout(key)[0]


def draw_page_fill(key, part):
    return layout(key)[1]


def draw_lengths(key, part):
    return layout(key)[2]


def draw_group_of_request(key, part):
    return layout(key)[3]


def draw_migrate_dest(key, part):
    subkeys = jax.random.split(jax.random.fold_in(key, 29), SPLITS)
    rows_dest = jax.vmap(lambda single: jax.random.permutation(single, POOL_DEV) // CAP)(subkeys)
    return rows_dest.reshape(NPAGES).astype(jnp.int32)


def draw_hidden_in(key, part):
    subkeys = jax.random.split(jax.random.fold_in(key, 3), 2)
    channel_ramp = 3.0 ** (jnp.arange(D, dtype=jnp.float32) / D)
    channel_rough = jnp.exp(jax.random.uniform(subkeys[1], (D,), jnp.float32, -0.7, 0.7))
    sample = jnp.clip(jax.random.normal(subkeys[0], (STEPS, REQ, D), jnp.float32), -6.0, 6.0)
    return (sample * channel_ramp * channel_rough).astype(jnp.bfloat16)


def draw_kv_pool(key, part):
    subkeys = jax.random.split(jax.random.fold_in(key, 5), 1)
    shape = (NPAGES, 2, PAGE, KV_HEADS * HEAD)
    return jnp.clip(jax.random.normal(subkeys[0], shape, jnp.float32), -6.0, 6.0).astype(jnp.bfloat16)


def block_scale(key, shape, cuts, least, top_value):
    level = 1.0
    for dim, shards_of in cuts:
        heights = jax.random.uniform(jax.random.fold_in(jax.random.fold_in(key, 6), dim), (shards_of,), jnp.float32, least / len(cuts), top_value / len(cuts))
        level = level * jnp.repeat(jnp.exp(heights), shape[dim] // shards_of).reshape((-1,) + (1,) * (len(shape) - 1 - dim))
    return level


def gaussian(rng, extent, spread, most, cuts=(), kind=jnp.bfloat16):
    factor_of = block_scale(rng, extent, cuts, -0.22, 0.18) if cuts else 1.0
    entries = jax.random.normal(rng, extent, jnp.float32) * spread * factor_of
    return jnp.minimum(jnp.maximum(entries, -most), most).astype(kind)


def setup_inputs(seed: int = 0) -> dict:
    streams_of = jax.random.split(jax.random.key(seed), 11)
    hidden_in = draw_hidden_in(jax.random.fold_in(streams_of[10], 71), 0)
    norm_gain = jnp.clip(1.0 + 0.18 * jax.random.normal(streams_of[1], (D,), jnp.float32), 0.099609375, 1.8984375).astype(jnp.bfloat16)
    w_qkv = gaussian(streams_of[2], (D, QKV_COLS), D ** -0.5, 0.0625, ((0, 4), (1, 8)))
    w_out = gaussian(streams_of[3], (HEADS * HEAD, D), (HEADS * HEAD) ** -0.5, 0.0625, ((0, 8), (1, 4)))
    kv_pool = draw_kv_pool(jax.random.fold_in(streams_of[10], 71), 0)
    page_owner = draw_page_owner(jax.random.fold_in(streams_of[10], 71), 0)
    page_fill = draw_page_fill(jax.random.fold_in(streams_of[10], 71), 0)
    lengths = draw_lengths(jax.random.fold_in(streams_of[10], 71), 0)
    group_of_request = draw_group_of_request(jax.random.fold_in(streams_of[10], 71), 0)
    migrate_dest = draw_migrate_dest(jax.random.fold_in(streams_of[10], 71), 0)
    return {"hidden_in": hidden_in, "norm_gain": norm_gain, "w_qkv": w_qkv, "w_out": w_out, "kv_pool": kv_pool, "page_owner": page_owner, "page_fill": page_fill, "lengths": lengths, "group_of_request": group_of_request, "migrate_dest": migrate_dest}


EPS = 1e-06
THETA = 1000000.0
NEG = -1e+30

def rotate(values, positions):
    half = values.shape[-1] // 2
    freq = THETA ** (-(jnp.arange(half, dtype=jnp.float32) * 2.0 / values.shape[-1]))
    angle = positions[..., None] * freq
    cosine = jnp.cos(angle)
    sine = jnp.sin(angle)
    first_half = values[..., :half]
    second_half = values[..., half:]
    return jnp.concatenate([first_half * cosine - second_half * sine, second_half * cosine + first_half * sine], -1)

def reference(hidden_in, norm_gain, w_qkv, w_out, kv_pool, page_owner, page_fill, lengths, group_of_request, migrate_dest):
    ratio = HEADS // KV_HEADS
    hidden_f = hidden_in.astype(jnp.float32)
    scale = lax.rsqrt(lax.optimization_barrier(jnp.mean(hidden_f * hidden_f, -1, keepdims=True)) + EPS)
    normed = (hidden_f * scale * norm_gain.astype(jnp.float32)).astype(jnp.bfloat16)
    projected = jnp.dot(normed.reshape(STEPS * REQ, D), w_qkv, preferred_element_type=jnp.float32).astype(jnp.bfloat16)
    projected = projected.reshape(STEPS, REQ, KV_HEADS, ratio + 2, HEAD)
    positions = (lengths[None, :] + jnp.arange(STEPS, dtype=jnp.int32)[:, None]).astype(jnp.float32)
    queries = rotate(projected[:, :, :, :ratio].astype(jnp.float32), positions[:, :, None, None]).astype(jnp.bfloat16)
    keys_new = rotate(projected[:, :, :, ratio].astype(jnp.float32), positions[:, :, None]).astype(jnp.bfloat16)
    values_new = projected[:, :, :, ratio + 1]
    new_kv = jnp.stack([keys_new.reshape(STEPS, REQ, KV_HEADS * HEAD), values_new.reshape(STEPS, REQ, KV_HEADS * HEAD)], 2)
    sorted_pages = jnp.argsort(page_owner, stable=True).astype(jnp.int32)
    padded = jnp.concatenate([sorted_pages, jnp.zeros((PROMPT_PAGES + OWN_PAGES,), jnp.int32)])
    causal = jnp.arange(STEPS)[None, :] <= jnp.arange(STEPS)[:, None]

    def pages_owned(owner, count):
        start = jnp.sum(page_owner < owner).astype(jnp.int32)
        live = jnp.sum(page_owner == owner).astype(jnp.int32)
        index = lax.dynamic_slice_in_dim(padded, start, count)
        slot_ok = jnp.arange(count) < live
        key_ok = slot_ok[:, None] & (jnp.arange(PAGE)[None, :] < page_fill[index][:, None])
        return (kv_pool[index], key_ok)

    def attend_request(request):
        group = group_of_request[request]
        shared, shared_ok = pages_owned(REQ + group, PROMPT_PAGES)
        owned, owned_ok = pages_owned(request, OWN_PAGES)
        pages = jnp.concatenate([shared, owned], 0)
        cache_ok = jnp.concatenate([shared_ok, owned_ok], 0).reshape(-1)
        key_rows = pages[:, 0].reshape(-1, KV_HEADS, HEAD)
        value_rows = pages[:, 1].reshape(-1, KV_HEADS, HEAD)
        key_rows = jnp.concatenate([key_rows, keys_new[:, request]], 0)
        value_rows = jnp.concatenate([value_rows, values_new[:, request]], 0)
        mask = jnp.concatenate([jnp.broadcast_to(cache_ok[None, :], (STEPS, cache_ok.shape[0])), causal], 1)
        query_rows = queries[:, request]
        scores = jnp.einsum('skqh,lkh->skql', query_rows.astype(jnp.float32), key_rows.astype(jnp.float32)) * HEAD ** (-0.5)
        mask = mask[:, None, None, :]
        scores = jnp.where(mask, scores, NEG)
        peak = lax.optimization_barrier(jnp.max(scores, -1, keepdims=True))
        expo = jnp.where(mask, jnp.exp(scores - peak), 0.0)
        totals = lax.optimization_barrier(jnp.sum(expo, -1))
        weights = expo.astype(jnp.bfloat16)
        summed = jnp.einsum('skql,lkh->skqh', weights.astype(jnp.float32), value_rows.astype(jnp.float32))
        result = (summed / totals[..., None]).astype(jnp.bfloat16)
        return result.reshape(STEPS, KV_HEADS * ratio * HEAD)
    attn = lax.map(attend_request, jnp.arange(REQ, dtype=jnp.int32))
    attn = attn.transpose(1, 0, 2).reshape(STEPS * REQ, HEADS * HEAD)
    layer_out = (jnp.dot(attn, w_out, preferred_element_type=jnp.float32) + hidden_f.reshape(STEPS * REQ, D)).astype(jnp.bfloat16)
    layer_out = layer_out.reshape(STEPS, REQ, D)
    blocks = migrate_dest.reshape(SPLITS, POOL_DEV)
    orders = jnp.argsort(blocks, axis=1, stable=True).astype(jnp.int32) + (jnp.arange(SPLITS, dtype=jnp.int32) * POOL_DEV)[:, None]
    arranged = orders.reshape(SPLITS, SPLITS, CAP).transpose(1, 0, 2).reshape(NPAGES)
    live_pool = jnp.where((page_owner >= 0)[:, None, None, None], kv_pool, jnp.zeros_like(kv_pool))
    new_pool = live_pool[arranged]
    return (layer_out, new_kv, new_pool)
```

```python
import jax
import jax.numpy as jnp
from jax import lax
from jax.sharding import PartitionSpec as P

HEADS = 64
KV_HEADS = 8
HEAD = 128
REQ = 48
GROUPS = 4
MEM = 16


EPS = 1e-06
THETA = 1000000.0
NEG = -1e30


def ring(axis, step):
    size = lax.axis_size(axis)
    return [(k, (k + step) % size) for k in range(size)]


def exchanged(parts, axis):
    size = lax.axis_size(axis)
    here = lax.axis_index(axis)
    return [
        lax.ppermute(
            lax.dynamic_index_in_dim(parts, (here + step) % size, 0, False), axis, ring(axis, step)
        )
        for step in range(1, size)
    ]


def collected(part, axis):
    size = lax.axis_size(axis)
    here = lax.axis_index(axis)
    ahead = [part] + [lax.ppermute(part, axis, ring(axis, size - step)) for step in range(1, size)]
    twice = jnp.stack(ahead + ahead[:-1])
    return lax.dynamic_slice_in_dim(twice, (size - here) % size, size, 0)


def pieces(value):
    high = lax.reduce_precision(value, 8, 7)
    middle = lax.reduce_precision(value - high, 8, 7)
    low = value - high - middle
    return [high.astype(jnp.bfloat16), middle.astype(jnp.bfloat16), low.astype(jnp.bfloat16)]


def whole(parts):
    return sum(part.astype(jnp.float32) for part in parts)


def packed(out, lse):
    count, rows = lse.shape
    tail = jnp.concatenate([p.reshape(count, rows // HEAD, HEAD) for p in pieces(lse)], 1)
    tail = jnp.pad(tail, ((0, 0), (0, 16 - tail.shape[1]), (0, 0)))
    return jnp.concatenate([out.astype(jnp.bfloat16), tail], 1)


def unpacked(both):
    rows = both.shape[0] - 16
    third = rows // HEAD
    lse = whole(
        [both[rows + k * third : rows + (k + 1) * third].reshape(rows) for k in range(3)]
    )
    return both[:rows].astype(jnp.float32), lse


def mixed(parts):
    peak = parts[0][1]
    for _, lse in parts[1:]:
        peak = jnp.maximum(peak, lse)
    fades = [jnp.exp(lse - peak) for _, lse in parts]
    total = sum(fades)
    value = sum(out * fade[..., None] for (out, _), fade in zip(parts, fades))
    return value / total[..., None], peak + jnp.log(total)


def rotate(values, cosine, sine):
    half = values.shape[-1] // 2
    first_half = values[..., :half]
    second_half = values[..., half:]
    return jnp.concatenate(
        [first_half * cosine - second_half * sine, second_half * cosine + first_half * sine], -1
    )


def body(
    hidden_in,
    norm_gain,
    w_qkv,
    w_out,
    kv_pool,
    page_owner,
    page_fill,
    lengths,
    group_of_request,
    migrate_dest,
):
    step_count, request_count, width_here = hidden_in.shape
    ratio = HEADS // KV_HEADS
    heads_here = w_qkv.shape[1] // ((ratio + 2) * HEAD)
    hidden_f = hidden_in.astype(jnp.float32)
    row_start = lax.axis_index("row") * width_here
    gain_f = lax.dynamic_slice_in_dim(norm_gain, row_start, width_here).astype(jnp.float32)
    width = width_here * lax.axis_size("row")
    squares = jnp.sum(hidden_f * hidden_f, -1)
    partial_value = jnp.dot(
        (hidden_f * gain_f).astype(jnp.bfloat16).reshape(step_count * request_count, width_here),
        w_qkv,
        preferred_element_type=jnp.float32,
    ).astype(jnp.bfloat16)
    columns = partial_value.shape[1]
    extra = jnp.pad(jnp.stack(pieces(squares), -1), ((0, 0), (0, 0), (0, HEAD - 3)))
    partial_value = jnp.concatenate(
        [partial_value.reshape(step_count, request_count, columns), extra], 2
    )
    step_here = lax.axis_index("row")
    position = (lengths + step_here).astype(jnp.float32)
    half = HEAD // 2
    angle = position[:, None] * THETA ** (-(jnp.arange(half, dtype=jnp.float32) * 2.0 / HEAD))
    cosine, sine = lax.optimization_barrier((jnp.cos(angle), jnp.sin(angle)))
    summed = lax.dynamic_index_in_dim(partial_value, step_here, 0, False).astype(jnp.float32)
    for part in exchanged(partial_value, "row"):
        summed = summed + part.astype(jnp.float32)
    scale = lax.rsqrt(jnp.sum(summed[:, columns : columns + 3], -1) / width + EPS)
    projected = (summed[:, :columns] * scale[:, None]).astype(jnp.bfloat16).astype(jnp.float32)
    projected = projected.reshape(request_count, heads_here * (ratio + 2), HEAD)
    rotated = rotate(projected, cosine[:, None], sine[:, None])
    is_value = jnp.arange(heads_here * (ratio + 2)) % (ratio + 2) == ratio + 1
    ready = jnp.where(is_value[None, :, None], projected, rotated).astype(jnp.bfloat16)
    ready = collected(ready, "row").reshape(
        step_count, request_count, heads_here, ratio + 2, HEAD
    )
    queries = ready[:, :, :, :ratio]
    keys_new = ready[:, :, :, ratio]
    values_new = ready[:, :, :, ratio + 1]
    local_req = request_count // lax.axis_size("seq")
    req_start = lax.axis_index("seq") * local_req
    new_kv = jnp.stack(
        [
            keys_new.reshape(step_count, request_count, heads_here * HEAD),
            values_new.reshape(step_count, request_count, heads_here * HEAD),
        ],
        2,
    )
    new_kv_local = lax.dynamic_slice_in_dim(new_kv, req_start, local_req, 1)
    device = lax.axis_index("row") * lax.axis_size("seq") + lax.axis_index("seq")
    pool_size = kv_pool.shape[0]
    page_len = kv_pool.shape[2]
    own_dest = lax.dynamic_slice_in_dim(migrate_dest, device * pool_size, pool_size)
    owners_here = lax.dynamic_slice_in_dim(page_owner, device * pool_size, pool_size)
    live_pages = jnp.where(
        (owners_here >= 0)[:, None, None, None], kv_pool, jnp.zeros_like(kv_pool)
    )
    send_order = jnp.argsort(own_dest, stable=True)
    moved = lax.all_to_all(
        live_pages[send_order], ("row", "seq"), split_axis=0, concat_axis=0, tiled=True
    )
    group_iota = jnp.arange(GROUPS, dtype=jnp.int32)
    belongs = group_of_request[None, :] == group_iota[:, None]
    member_rank = jnp.cumsum(belongs.astype(jnp.int32), 1) - 1
    slot_hit = belongs[:, None, :] & (
        member_rank[:, None, :] == jnp.arange(MEM, dtype=jnp.int32)[None, :, None]
    )
    member_ok = jnp.any(slot_hit, -1)
    members = jnp.sum(jnp.where(slot_hit, jnp.arange(request_count, dtype=jnp.int32), 0), -1)
    member_id = jnp.where(member_ok, members, -1)
    row_count = MEM * step_count * ratio
    grouped_q = (
        queries[:, members].transpose(1, 3, 2, 0, 4, 5).reshape(GROUPS, heads_here, row_count, HEAD)
    )
    fills = lax.dynamic_slice_in_dim(page_fill, device * pool_size, pool_size)
    live_count = jnp.sum((owners_here >= 0).astype(jnp.int32))
    block_pages = min(16, pool_size)
    trips = (live_count + block_pages - 1) // block_pages
    page_group = jnp.where(
        owners_here >= REQ, owners_here - REQ, group_of_request[jnp.clip(owners_here, 0, REQ - 1)]
    )
    page_group = jnp.clip(page_group, 0, GROUPS - 1)
    slot_ok = (
        member_ok[page_group]
        & (owners_here >= 0)[:, None]
        & ((owners_here >= REQ)[:, None] | (member_id[page_group] == owners_here[:, None]))
    )
    row_ok = jnp.repeat(slot_ok, step_count * ratio, axis=1)
    key_ok = jnp.arange(page_len)[None, :] < fills[:, None]
    score_scale = HEAD ** (-0.5)

    def visit_block(number, carry):
        running_max, running_sum, weighted = carry
        first = number * block_pages
        chosen = lax.dynamic_slice_in_dim(kv_pool, first, block_pages, 0)
        groups_here = lax.dynamic_slice_in_dim(page_group, first, block_pages, 0)
        rows_fine = lax.dynamic_slice_in_dim(row_ok, first, block_pages, 0)
        keys_fine = lax.dynamic_slice_in_dim(key_ok, first, block_pages, 0)
        key_block = chosen[:, 0].reshape(block_pages, page_len, heads_here, HEAD)
        value_block = chosen[:, 1].reshape(block_pages, page_len, heads_here, HEAD)
        query_block = grouped_q[groups_here]
        scores = (
            jnp.einsum(
                "pkrh,ptkh->pkrt", query_block, key_block, preferred_element_type=jnp.float32
            )
            * score_scale
        )
        mask = rows_fine[:, None, :, None] & keys_fine[:, None, None, :]
        scores = jnp.where(mask, scores, NEG)
        page_max = jnp.max(scores, -1)
        group_hit = groups_here[:, None] == group_iota[None, :]
        block_max = jnp.max(jnp.where(group_hit[:, :, None, None], page_max[:, None], NEG), 0)
        new_max = jnp.maximum(running_max, block_max)
        expo = jnp.where(mask, jnp.exp(scores - new_max[groups_here][..., None]), 0.0)
        weights = expo.astype(jnp.bfloat16)
        value_sums = jnp.einsum(
            "pkrt,ptkh->pkrh", weights, value_block, preferred_element_type=jnp.float32
        )
        hit_float = group_hit.astype(jnp.float32)
        fade = jnp.exp(running_max - new_max)
        running_sum = running_sum * fade + jnp.einsum(
            "pg,pkr->gkr", hit_float, jnp.sum(expo, -1), precision=lax.Precision.HIGHEST
        )
        weighted = weighted * fade[..., None] + jnp.einsum(
            "pg,pkrh->gkrh", hit_float, value_sums, precision=lax.Precision.HIGHEST
        )
        return (new_max, running_sum, weighted)

    initial = (
        jnp.full((GROUPS, heads_here, row_count), NEG, jnp.float32),
        jnp.zeros((GROUPS, heads_here, row_count), jnp.float32),
        jnp.zeros((GROUPS, heads_here, row_count, HEAD), jnp.float32),
    )
    carried = lax.fori_loop(0, trips, visit_block, initial)
    run_max, run_sum, run_acc = carried
    slot_of = group_of_request * MEM + member_rank[group_of_request, jnp.arange(request_count)]
    rows_here = step_count * ratio
    held = run_sum > 0
    out_part = run_acc / jnp.where(held, run_sum, 1.0)[..., None]
    lse_part = jnp.where(held, run_max + jnp.log(jnp.where(held, run_sum, 1.0)), NEG)
    out_part = out_part.reshape(GROUPS * MEM, rows_here, HEAD)[slot_of]
    lse_part = lse_part.reshape(GROUPS * MEM, rows_here)[slot_of]
    seq_size = lax.axis_size("seq")
    own_rows = local_req * rows_here
    both = packed(
        out_part.reshape(seq_size, own_rows, HEAD), lse_part.reshape(seq_size, own_rows)
    )
    parts = [lax.dynamic_index_in_dim(both, lax.axis_index("seq"), 0, False)]
    parts += exchanged(both, "seq")
    out_part, lse_part = mixed([unpacked(part) for part in parts])
    both = packed(out_part[None], lse_part[None])[0]
    parts = [both] + [lax.ppermute(both, "row", ring("row", k)) for k in range(1, 4)]
    query_own = lax.dynamic_slice_in_dim(queries, req_start, local_req, 1)[:, :, 0]
    key_own = lax.dynamic_slice_in_dim(keys_new, req_start, local_req, 1)[:, :, 0]
    value_own = lax.dynamic_slice_in_dim(values_new, req_start, local_req, 1)[:, :, 0]
    fresh = (
        jnp.einsum("sjqh,ujh->jsqu", query_own, key_own, preferred_element_type=jnp.float32)
        * score_scale
    )
    causal = (jnp.arange(step_count)[None, :] <= jnp.arange(step_count)[:, None])[:, None]
    fresh = jnp.where(causal, fresh, NEG)
    fresh_max = jnp.max(fresh, -1)
    expo_new = jnp.where(causal, jnp.exp(fresh - fresh_max[..., None]), 0.0)
    fresh_sum = jnp.sum(expo_new, -1)
    fresh_out = jnp.einsum(
        "jsqu,ujh->jsqh",
        expo_new.astype(jnp.bfloat16),
        value_own,
        preferred_element_type=jnp.float32,
    )
    fresh_part = (
        (fresh_out / fresh_sum[..., None]).reshape(own_rows, HEAD),
        (fresh_max + jnp.log(fresh_sum)).reshape(own_rows),
    )
    attn, _ = mixed([fresh_part] + [unpacked(part) for part in parts])
    picked = (
        attn.astype(jnp.bfloat16)
        .reshape(local_req, step_count, ratio * HEAD)
        .transpose(1, 0, 2)
        .reshape(step_count * local_req, heads_here * ratio * HEAD)
    )
    partial_out = jnp.dot(picked, w_out, preferred_element_type=jnp.float32).astype(jnp.bfloat16)
    col_size = lax.axis_size("col")
    col_width = partial_out.shape[1] // col_size
    spread = partial_out.reshape(step_count * local_req, col_size, col_width).transpose(1, 0, 2)
    summed = jnp.sum(
        lax.all_to_all(spread, "col", 0, 0, tiled=True).astype(jnp.float32), 0
    )
    residual = lax.dynamic_slice_in_dim(
        lax.dynamic_slice_in_dim(hidden_f, req_start, local_req, 1),
        lax.axis_index("col") * col_width,
        col_width,
        2,
    )
    layer_out = (summed.reshape(step_count, local_req, col_width) + residual).astype(jnp.bfloat16)
    return (layer_out, new_kv_local, moved)


def solution(mesh):
    in_specs = (
        P(None, None, "row"),
        P(),
        P("row", "col"),
        P("col", "row"),
        P(("row", "seq"), None, None, "col"),
        P(),
        P(),
        P(),
        P(),
        P(),
    )
    out_specs = (
        P(None, "seq", ("row", "col")),
        P(None, "seq", None, "col"),
        P(("row", "seq"), None, None, "col"),
    )
    return jax.shard_map(body, mesh=mesh, in_specs=in_specs, out_specs=out_specs, check_vma=False)
```

```python
import functools

import jax
import jax.numpy as jnp
from jax import lax
from jax.experimental import pallas as pl
from jax.experimental.pallas import tpu as pltpu
from jax.sharding import PartitionSpec as P

HEADS = 64
KV_HEADS = 8
HEAD = 128
REQ = 48
GROUPS = 4
MEM = 16


EPS = 1e-06
THETA = 1000000.0
NEG = -1e30


def ring(axis, step):
    size = lax.axis_size(axis)
    return [(k, (k + step) % size) for k in range(size)]


def exchanged(parts, axis):
    size = lax.axis_size(axis)
    here = lax.axis_index(axis)
    return [
        lax.ppermute(
            lax.dynamic_index_in_dim(parts, (here + step) % size, 0, False), axis, ring(axis, step)
        )
        for step in range(1, size)
    ]


def collected(part, axis):
    size = lax.axis_size(axis)
    here = lax.axis_index(axis)
    ahead = [part] + [lax.ppermute(part, axis, ring(axis, size - step)) for step in range(1, size)]
    twice = jnp.stack(ahead + ahead[:-1])
    return lax.dynamic_slice_in_dim(twice, (size - here) % size, size, 0)


def pieces(value):
    high = lax.reduce_precision(value, 8, 7)
    middle = lax.reduce_precision(value - high, 8, 7)
    low = value - high - middle
    return [high.astype(jnp.bfloat16), middle.astype(jnp.bfloat16), low.astype(jnp.bfloat16)]


def packed_tail(lse_rows):
    count = len(lse_rows)
    row = lax.broadcasted_iota(jnp.int32, (16, HEAD), 0)
    tail = jnp.zeros((16, HEAD), jnp.float32)
    for index, lse in enumerate(lse_rows):
        high = lse.astype(jnp.bfloat16).astype(jnp.float32)
        middle = (lse - high).astype(jnp.bfloat16).astype(jnp.float32)
        low = lse - high - middle
        for k, term in enumerate((high, middle, low)):
            tail = jnp.where(row == k * count + index, jnp.broadcast_to(term, (16, HEAD)), tail)
    return tail.astype(jnp.bfloat16)


def attend_kernel(seqs, table, q_ref, pool_ref, out_ref, grouped, gathered, lse_rows, acc):
    page_len = pool_ref.shape[2]
    limit = pool_ref.shape[0]
    rows_each = q_ref.shape[1]
    requests = q_ref.shape[0]
    row_count = MEM * rows_each
    at_fill, at_code, at_start, at_slot = limit, 2 * limit, 3 * limit, 3 * limit + 8
    factor = HEAD ** (-0.5)
    grouped[...] = jnp.zeros_like(grouped)
    for r in range(requests):
        slot = table[at_slot + r]
        grouped[pl.ds(pl.multiple_of(slot * rows_each, rows_each), rows_each), :] = q_ref[r]
    lane_slot = lax.broadcasted_iota(jnp.int32, (1, row_count), 1) // rows_each
    token = lax.broadcasted_iota(jnp.int32, (page_len, row_count), 0)
    for g in range(GROUPS):
        first = table[at_start + g]
        last = table[at_start + g + 1]
        acc[...] = jnp.zeros_like(acc)

        def visit(number, carry):
            old_max, old_sum = carry
            base = first + number * TILE
            places = [jnp.minimum(base + i, limit - 1) for i in range(TILE)]
            keys = jnp.concatenate([pool_ref[table[p], 0] for p in places], 0)
            values = jnp.concatenate([pool_ref[table[p], 1] for p in places], 0)
            scores = lax.dot_general(
                keys,
                grouped[pl.ds(g * row_count, row_count), :],
                (((1,), (1,)), ((), ())),
                preferred_element_type=jnp.float32,
            )
            shown = []
            for i, p in enumerate(places):
                fill = jnp.where(base + i < last, table[at_fill + p], 0)
                code = table[at_code + p]
                rows_ok = jnp.where((lane_slot == code) | (code < 0), fill, 0)
                part = scores[i * page_len : (i + 1) * page_len]
                shown.append(jnp.where(token < rows_ok, part, NEG))
            new_max = old_max
            for part in shown:
                new_max = jnp.maximum(new_max, jnp.max(part, 0, keepdims=True))
            base_max = jnp.where(new_max > 0.5 * NEG, new_max, 0.0)
            fade = jnp.exp((old_max - base_max) * factor)
            expo = [jnp.exp((part - base_max) * factor) for part in shown]
            new_sum = old_sum * fade
            for part in expo:
                new_sum = new_sum + jnp.sum(part, 0, keepdims=True)
            weights = jnp.concatenate([part.astype(jnp.bfloat16) for part in expo], 0)
            acc[...] = acc[...] * fade + lax.dot_general(
                values, weights, (((0,), (0,)), ((), ())), preferred_element_type=jnp.float32
            )
            return new_max, new_sum

        start = (
            jnp.full((1, row_count), NEG, jnp.float32),
            jnp.zeros((1, row_count), jnp.float32),
        )
        run_max, run_sum = lax.fori_loop(0, (last - first + TILE - 1) // TILE, visit, start)
        held = run_sum > 0
        safe = jnp.where(held, run_sum, 1.0)
        lse = jnp.where(held, run_max * factor + jnp.log(safe), NEG)
        gathered[pl.ds(g * row_count, row_count), :] = (acc[...] * (1.0 / safe)).T
        for k in range(row_count // HEAD):
            lse_rows[pl.ds(g * (row_count // HEAD) + k, 1), :] = lse[:, k * HEAD : (k + 1) * HEAD]
    lane = lax.broadcasted_iota(jnp.int32, (8, HEAD), 1) // rows_each
    each = requests // seqs
    per_row = HEAD // rows_each
    for s in range(seqs):
        tails = []
        for k in range(each // per_row):
            line = jnp.zeros((8, HEAD), jnp.float32)
            for i in range(per_row):
                r = s * each + k * per_row + i
                slot = table[at_slot + r]
                out_ref[s, pl.ds((k * per_row + i) * rows_each, rows_each), :] = gathered[
                    pl.ds(pl.multiple_of(slot * rows_each, rows_each), rows_each), :
                ].astype(jnp.bfloat16)
                source = jnp.broadcast_to(lse_rows[pl.ds(slot // per_row, 1), :], (8, HEAD))
                shift = lax.rem(i - lax.rem(slot, per_row) + per_row, per_row) * rows_each
                line = jnp.where(lane == i, pltpu.roll(source, shift, 1), line)
            tails.append(line[0:1])
        out_ref[s, pl.ds(each * rows_each, 16), :] = packed_tail(tails)


TILE = 4


def attend(table, queries, pool, seqs):
    requests, rows_each, _ = queries.shape
    limit = pool.shape[0] // 2
    own = requests // seqs * rows_each
    return pl.pallas_call(
        functools.partial(attend_kernel, seqs),
        out_shape=jax.ShapeDtypeStruct((seqs, own + 16, HEAD), jnp.bfloat16),
        grid_spec=pltpu.PrefetchScalarGridSpec(
            num_scalar_prefetch=1,
            grid=(1,),
            in_specs=[
                pl.BlockSpec((requests, rows_each, HEAD), lambda i, t: (0, 0, 0)),
                pl.BlockSpec((limit,) + pool.shape[1:], lambda i, t: (0, 0, 0, 0)),
            ],
            out_specs=pl.BlockSpec((seqs, own + 16, HEAD), lambda i, t: (0, 0, 0)),
            scratch_shapes=[
                pltpu.VMEM((GROUPS * MEM * rows_each, HEAD), jnp.bfloat16),
                pltpu.VMEM((GROUPS * MEM * rows_each, HEAD), jnp.float32),
                pltpu.VMEM((GROUPS * MEM * rows_each // HEAD, HEAD), jnp.float32),
                pltpu.VMEM((HEAD, MEM * rows_each), jnp.float32),
            ],
        ),
        cost_estimate=pl.CostEstimate(
            flops=4 * limit * 64 * MEM * rows_each * HEAD,
            bytes_accessed=limit * 2 * 64 * HEAD * 2,
            transcendentals=limit * 64 * MEM * rows_each,
        ),
        name="attend",
    )(table, queries, pool)


def fresh_kernel(steps, q_ref, k_ref, v_ref, out_ref):
    rows = q_ref.shape[0]
    count = k_ref.shape[0] // steps
    rows_each = rows // count
    shape = (steps * count, rows)
    key = lax.broadcasted_iota(jnp.int32, shape, 0)
    lane = lax.broadcasted_iota(jnp.int32, shape, 1)
    seen = (lane // rows_each == lax.rem(key, count)) & (
        key // count <= lax.rem(lane, rows_each) // (rows_each // steps)
    )
    scores = lax.dot_general(
        k_ref[...], q_ref[...], (((1,), (1,)), ((), ())), preferred_element_type=jnp.float32
    ) * HEAD ** (-0.5)
    scores = jnp.where(seen, scores, NEG)
    peak = jnp.max(scores, 0, keepdims=True)
    expo = jnp.where(seen, jnp.exp(scores - peak), 0.0)
    total = jnp.sum(expo, 0, keepdims=True)
    value = lax.dot_general(
        v_ref[...],
        expo.astype(jnp.bfloat16),
        (((0,), (0,)), ((), ())),
        preferred_element_type=jnp.float32,
    )
    out_ref[pl.ds(0, rows), :] = (value * (1.0 / total)).T.astype(jnp.bfloat16)
    lse = peak + jnp.log(total)
    out_ref[pl.ds(rows, 16), :] = packed_tail(
        [lse[:, k * HEAD : (k + 1) * HEAD] for k in range(rows // HEAD)]
    )


def fresh_part(queries, keys, values, steps):
    rows = queries.shape[0]
    return pl.pallas_call(
        functools.partial(fresh_kernel, steps),
        out_shape=jax.ShapeDtypeStruct((rows + 16, HEAD), jnp.bfloat16),
        cost_estimate=pl.CostEstimate(
            flops=4 * rows * keys.shape[0] * HEAD, bytes_accessed=rows * HEAD * 4, transcendentals=0
        ),
        name="fresh",
    )(queries, keys, values)


def mix_refs(parts):
    rows = parts[0].shape[0] - 16
    blocks = rows // HEAD
    lses = []
    for part in parts:
        tail = part[pl.ds(rows, 16), :].astype(jnp.float32)
        lses.append(
            tail[0:blocks] + tail[blocks : 2 * blocks] + tail[2 * blocks : 3 * blocks]
        )
    peak = lses[0]
    for lse in lses[1:]:
        peak = jnp.maximum(peak, lse)
    fades = [jnp.exp(lse - peak) for lse in lses]
    total = sum(fades)
    inverse = 1.0 / total
    turned = [
        jnp.concatenate([fade * inverse, jnp.zeros((8 - blocks, HEAD), jnp.float32)], 0).T
        for fade in fades
    ]
    values = []
    for k in range(blocks):
        value = 0.0
        for part, weight in zip(parts, turned):
            value = value + part[pl.ds(k * HEAD, HEAD), :].astype(jnp.float32) * weight[:, k : k + 1]
        values.append(value)
    return values, peak + jnp.log(total)


def mix_kernel(*refs):
    out_ref = refs[-1]
    values, lse = mix_refs(refs[:-1])
    for k, value in enumerate(values):
        out_ref[pl.ds(k * HEAD, HEAD), :] = value.astype(jnp.bfloat16)
    out_ref[pl.ds(len(values) * HEAD, 16), :] = packed_tail(
        [lse[k : k + 1] for k in range(len(values))]
    )


def mix(parts):
    return pl.pallas_call(
        mix_kernel,
        out_shape=jax.ShapeDtypeStruct(parts[0].shape, jnp.bfloat16),
        cost_estimate=pl.CostEstimate(
            flops=2 * len(parts) * parts[0].size, bytes_accessed=parts[0].size * 10, transcendentals=0
        ),
        name="mix",
    )(*parts)


def final_kernel(ratio, *refs):
    parts, out_ref, scratch = refs[:-2], refs[-2], refs[-1]
    values, _ = mix_refs(parts)
    for k, value in enumerate(values):
        scratch[pl.ds(k * HEAD, HEAD), :] = value
    tokens = out_ref.shape[0]
    for h in range(ratio):
        out_ref[:, h * HEAD : (h + 1) * HEAD] = scratch[pl.ds(h, tokens, stride=ratio), :].astype(
            jnp.bfloat16
        )


def final(parts, ratio):
    rows = parts[0].shape[0] - 16
    return pl.pallas_call(
        functools.partial(final_kernel, ratio),
        out_shape=jax.ShapeDtypeStruct((rows // ratio, ratio * HEAD), jnp.bfloat16),
        scratch_shapes=[pltpu.VMEM((rows, HEAD), jnp.float32)],
        cost_estimate=pl.CostEstimate(
            flops=2 * len(parts) * parts[0].size, bytes_accessed=parts[0].size * 10, transcendentals=0
        ),
        name="final",
    )(*parts)


def page_table(owners, fills, group_of_request):
    requests = group_of_request.shape[0]
    count = owners.shape[0]
    index = jnp.arange(requests, dtype=jnp.int32)
    same = group_of_request[:, None] == group_of_request[None, :]
    rank = jnp.sum((same & (index[None, :] < index[:, None])).astype(jnp.int32), 1)
    slot = group_of_request * MEM + rank
    shared = owners >= requests
    own_slot = jnp.sum(jnp.where(owners[:, None] == index[None, :], slot[None, :], 0), 1)
    group = jnp.where(shared, owners - requests, own_slot // MEM)
    group = jnp.where(owners >= 0, group, GROUPS)
    code = jnp.where(shared, -1, own_slot % MEM)
    place = jnp.arange(count, dtype=jnp.int32)
    before = (group[None, :] < group[:, None]) | (
        (group[None, :] == group[:, None]) & (place[None, :] < place[:, None])
    )
    target = jnp.sum(before.astype(jnp.int32), 1)
    hit = target[None, :] == place[:, None]
    ordered = [
        jnp.sum(jnp.where(hit, row[None, :], 0), 1) for row in (place, fills, code)
    ]
    starts = jnp.sum(
        (group[None, :] < jnp.arange(8, dtype=jnp.int32)[:, None]).astype(jnp.int32), 1
    )
    return jnp.concatenate(ordered + [starts, slot])


def rotate(values, cosine, sine):
    half = values.shape[-1] // 2
    first_half = values[..., :half]
    second_half = values[..., half:]
    return jnp.concatenate(
        [first_half * cosine - second_half * sine, second_half * cosine + first_half * sine], -1
    )


def body(
    hidden_in,
    norm_gain,
    w_qkv,
    w_out,
    kv_pool,
    page_owner,
    page_fill,
    lengths,
    group_of_request,
    migrate_dest,
):
    step_count, request_count, width_here = hidden_in.shape
    ratio = HEADS // KV_HEADS
    heads_here = w_qkv.shape[1] // ((ratio + 2) * HEAD)
    hidden_f = hidden_in.astype(jnp.float32)
    row_start = lax.axis_index("row") * width_here
    gain_f = lax.dynamic_slice_in_dim(norm_gain, row_start, width_here).astype(jnp.float32)
    width = width_here * lax.axis_size("row")
    squares = jnp.sum(hidden_f * hidden_f, -1)
    partial_value = jnp.dot(
        (hidden_f * gain_f).astype(jnp.bfloat16).reshape(step_count * request_count, width_here),
        w_qkv,
        preferred_element_type=jnp.float32,
    ).astype(jnp.bfloat16)
    columns = partial_value.shape[1]
    extra = jnp.pad(jnp.stack(pieces(squares), -1), ((0, 0), (0, 0), (0, HEAD - 3)))
    partial_value = jnp.concatenate(
        [partial_value.reshape(step_count, request_count, columns), extra], 2
    )
    step_here = lax.axis_index("row")
    position = (lengths + step_here).astype(jnp.float32)
    half = HEAD // 2
    angle = position[:, None] * THETA ** (-(jnp.arange(half, dtype=jnp.float32) * 2.0 / HEAD))
    cosine, sine = lax.optimization_barrier((jnp.cos(angle), jnp.sin(angle)))
    summed = lax.dynamic_index_in_dim(partial_value, step_here, 0, False).astype(jnp.float32)
    for part in exchanged(partial_value, "row"):
        summed = summed + part.astype(jnp.float32)
    scale = lax.rsqrt(jnp.sum(summed[:, columns : columns + 3], -1) / width + EPS)
    projected = (summed[:, :columns] * scale[:, None]).astype(jnp.bfloat16).astype(jnp.float32)
    projected = projected.reshape(request_count, heads_here * (ratio + 2), HEAD)
    rotated = rotate(projected, cosine[:, None], sine[:, None])
    is_value = jnp.arange(heads_here * (ratio + 2)) % (ratio + 2) == ratio + 1
    ready = jnp.where(is_value[None, :, None], projected, rotated).astype(jnp.bfloat16)
    ready = collected(ready, "row").reshape(
        step_count, request_count, heads_here, ratio + 2, HEAD
    )
    queries = ready[:, :, :, :ratio]
    keys_new = ready[:, :, :, ratio]
    values_new = ready[:, :, :, ratio + 1]
    local_req = request_count // lax.axis_size("seq")
    req_start = lax.axis_index("seq") * local_req
    new_kv = jnp.stack(
        [
            keys_new.reshape(step_count, request_count, heads_here * HEAD),
            values_new.reshape(step_count, request_count, heads_here * HEAD),
        ],
        2,
    )
    new_kv_local = lax.dynamic_slice_in_dim(new_kv, req_start, local_req, 1)
    device = lax.axis_index("row") * lax.axis_size("seq") + lax.axis_index("seq")
    pool_size = kv_pool.shape[0]
    page_len = kv_pool.shape[2]
    own_dest = lax.dynamic_slice_in_dim(migrate_dest, device * pool_size, pool_size)
    owners_here = lax.dynamic_slice_in_dim(page_owner, device * pool_size, pool_size)
    send_order = jnp.argsort(own_dest, stable=True)
    moved = lax.all_to_all(
        kv_pool[send_order], ("row", "seq"), split_axis=0, concat_axis=0, tiled=True
    )
    splits = page_owner.shape[0] // pool_size
    coming = ((page_owner >= 0) & (migrate_dest == device)).reshape(splits, pool_size)
    live_from = jnp.sum(coming.astype(jnp.int32), 1)
    cap = pool_size // splits
    full = jnp.arange(cap, dtype=jnp.int32)[None, :] < live_from[:, None]
    moved = jnp.where(full.reshape(pool_size)[:, None, None, None], moved, jnp.zeros_like(moved))
    fills = lax.dynamic_slice_in_dim(page_fill, device * pool_size, pool_size)
    live_limit = pool_size // 2
    table = page_table(owners_here[:live_limit], fills[:live_limit], group_of_request)
    rows_here = step_count * ratio
    rows_first = queries[:, :, 0].transpose(1, 0, 2, 3).reshape(request_count, rows_here, HEAD)
    seq_size = lax.axis_size("seq")
    own_rows = local_req * rows_here
    both = attend(table, rows_first, kv_pool, seq_size)
    parts = [lax.dynamic_index_in_dim(both, lax.axis_index("seq"), 0, False)]
    both = mix(parts + exchanged(both, "seq"))
    parts = [both] + [lax.ppermute(both, "row", ring("row", k)) for k in range(1, 4)]
    query_own = lax.dynamic_slice_in_dim(rows_first, req_start, local_req, 0)
    key_own = lax.dynamic_slice_in_dim(keys_new, req_start, local_req, 1)
    value_own = lax.dynamic_slice_in_dim(values_new, req_start, local_req, 1)
    own = fresh_part(
        query_own.reshape(own_rows, HEAD),
        key_own.reshape(step_count * local_req, HEAD),
        value_own.reshape(step_count * local_req, HEAD),
        step_count,
    )
    picked = final([own] + parts, ratio)
    partial_out = jnp.dot(picked, w_out, preferred_element_type=jnp.float32).astype(jnp.bfloat16)
    col_size = lax.axis_size("col")
    col_width = partial_out.shape[1] // col_size
    spread = partial_out.reshape(step_count * local_req, col_size, col_width).transpose(1, 0, 2)
    summed = jnp.sum(
        lax.all_to_all(spread, "col", 0, 0, tiled=True).astype(jnp.float32), 0
    )
    residual = lax.dynamic_slice_in_dim(
        lax.dynamic_slice_in_dim(hidden_f, req_start, local_req, 1),
        lax.axis_index("col") * col_width,
        col_width,
        2,
    )
    summed = summed.reshape(local_req, step_count, col_width).transpose(1, 0, 2)
    layer_out = (summed + residual).astype(jnp.bfloat16)
    return (layer_out, new_kv_local, moved)


def solution(mesh):
    in_specs = (
        P(None, None, "row"),
        P(),
        P("row", "col"),
        P("col", "row"),
        P(("row", "seq"), None, None, "col"),
        P(),
        P(),
        P(),
        P(),
        P(),
    )
    out_specs = (
        P(None, "seq", ("row", "col")),
        P(None, "seq", None, "col"),
        P(("row", "seq"), None, None, "col"),
    )
    return jax.shard_map(body, mesh=mesh, in_specs=in_specs, out_specs=out_specs, check_vma=False)
```

```python
import functools

import jax
import jax.numpy as jnp
from jax import lax
from jax.experimental import pallas as pl
from jax.experimental.pallas import tpu as pltpu
from jax.sharding import PartitionSpec as P

HEADS = 64
KV_HEADS = 8
HEAD = 128
GROUPS = 4
MEM = 16


EPS = 1e-06
THETA = 1000000.0
NEG = -1e30


def ring(axis, step):
    size = lax.axis_size(axis)
    return [(k, (k + step) % size) for k in range(size)]


def exchanged(parts, axis):
    size = lax.axis_size(axis)
    here = lax.axis_index(axis)
    return [
        lax.ppermute(
            lax.dynamic_index_in_dim(parts, (here + step) % size, 0, False), axis, ring(axis, step)
        )
        for step in range(1, size)
    ]


def collected(part, axis):
    size = lax.axis_size(axis)
    here = lax.axis_index(axis)
    ahead = [part] + [lax.ppermute(part, axis, ring(axis, size - step)) for step in range(1, size)]
    twice = jnp.stack(ahead + ahead[:-1])
    return lax.dynamic_slice_in_dim(twice, (size - here) % size, size, 0)


def pieces(value):
    high = lax.reduce_precision(value, 8, 7)
    middle = lax.reduce_precision(value - high, 8, 7)
    low = value - high - middle
    return [high.astype(jnp.bfloat16), middle.astype(jnp.bfloat16), low.astype(jnp.bfloat16)]


def packed_tail(lse_rows):
    count = len(lse_rows)
    row = lax.broadcasted_iota(jnp.int32, (16, HEAD), 0)
    tail = jnp.zeros((16, HEAD), jnp.float32)
    for index, lse in enumerate(lse_rows):
        high = lse.astype(jnp.bfloat16).astype(jnp.float32)
        middle = (lse - high).astype(jnp.bfloat16).astype(jnp.float32)
        low = lse - high - middle
        for k, term in enumerate((high, middle, low)):
            tail = jnp.where(row == k * count + index, jnp.broadcast_to(term, (16, HEAD)), tail)
    return tail.astype(jnp.bfloat16)


def attend_kernel(seqs, table, q_ref, pool_ref, out_ref, grouped, gathered, lse_rows, acc):
    page_len = pool_ref.shape[2]
    limit = pool_ref.shape[0]
    rows_each = q_ref.shape[1]
    requests = q_ref.shape[0]
    row_count = MEM * rows_each
    at_fill, at_code, at_start, at_slot = limit, 2 * limit, 3 * limit, 3 * limit + 8
    factor = HEAD ** (-0.5)
    grouped[...] = jnp.zeros_like(grouped)
    for r in range(requests):
        slot = table[at_slot + r]
        grouped[pl.ds(pl.multiple_of(slot * rows_each, rows_each), rows_each), :] = q_ref[r]
    lane_slot = lax.broadcasted_iota(jnp.int32, (1, row_count), 1) // rows_each
    token = lax.broadcasted_iota(jnp.int32, (page_len, row_count), 0)
    for g in range(GROUPS):
        first = table[at_start + g]
        last = table[at_start + g + 1]
        acc[...] = jnp.zeros_like(acc)

        def visit(number, carry):
            old_max, old_sum = carry
            base = first + number * TILE
            places = [jnp.minimum(base + i, limit - 1) for i in range(TILE)]
            keys = jnp.concatenate([pool_ref[table[p], 0] for p in places], 0)
            values = jnp.concatenate([pool_ref[table[p], 1] for p in places], 0)
            scores = lax.dot_general(
                keys,
                grouped[pl.ds(g * row_count, row_count), :],
                (((1,), (1,)), ((), ())),
                preferred_element_type=jnp.float32,
            )
            shown = []
            for i, p in enumerate(places):
                fill = jnp.where(base + i < last, table[at_fill + p], 0)
                code = table[at_code + p]
                rows_ok = jnp.where((lane_slot == code) | (code < 0), fill, 0)
                part = scores[i * page_len : (i + 1) * page_len]
                shown.append(jnp.where(token < rows_ok, part, NEG))
            new_max = old_max
            for part in shown:
                new_max = jnp.maximum(new_max, jnp.max(part, 0, keepdims=True))
            base_max = jnp.where(new_max > 0.5 * NEG, new_max, 0.0)
            fade = jnp.exp((old_max - base_max) * factor)
            expo = [jnp.exp((part - base_max) * factor) for part in shown]
            new_sum = old_sum * fade
            for part in expo:
                new_sum = new_sum + jnp.sum(part, 0, keepdims=True)
            weights = jnp.concatenate([part.astype(jnp.bfloat16) for part in expo], 0)
            acc[...] = acc[...] * fade + lax.dot_general(
                values, weights, (((0,), (0,)), ((), ())), preferred_element_type=jnp.float32
            )
            return new_max, new_sum

        start = (
            jnp.full((1, row_count), NEG, jnp.float32),
            jnp.zeros((1, row_count), jnp.float32),
        )
        run_max, run_sum = lax.fori_loop(0, (last - first + TILE - 1) // TILE, visit, start)
        held = run_sum > 0
        safe = jnp.where(held, run_sum, 1.0)
        lse = jnp.where(held, run_max * factor + jnp.log(safe), NEG)
        gathered[pl.ds(g * row_count, row_count), :] = (acc[...] * (1.0 / safe)).T
        for k in range(row_count // HEAD):
            lse_rows[pl.ds(g * (row_count // HEAD) + k, 1), :] = lse[:, k * HEAD : (k + 1) * HEAD]
    lane = lax.broadcasted_iota(jnp.int32, (8, HEAD), 1) // rows_each
    each = requests // seqs
    per_row = HEAD // rows_each
    for s in range(seqs):
        tails = []
        for k in range(each // per_row):
            line = jnp.zeros((8, HEAD), jnp.float32)
            for i in range(per_row):
                r = s * each + k * per_row + i
                slot = table[at_slot + r]
                out_ref[s, pl.ds((k * per_row + i) * rows_each, rows_each), :] = gathered[
                    pl.ds(pl.multiple_of(slot * rows_each, rows_each), rows_each), :
                ].astype(jnp.bfloat16)
                source = jnp.broadcast_to(lse_rows[pl.ds(slot // per_row, 1), :], (8, HEAD))
                shift = lax.rem(i - lax.rem(slot, per_row) + per_row, per_row) * rows_each
                line = jnp.where(lane == i, pltpu.roll(source, shift, 1), line)
            tails.append(line[0:1])
        out_ref[s, pl.ds(each * rows_each, 16), :] = packed_tail(tails)


TILE = 4


def attend(table, queries, pool, seqs):
    requests, rows_each, _ = queries.shape
    limit = pool.shape[0] // 2
    own = requests // seqs * rows_each
    return pl.pallas_call(
        functools.partial(attend_kernel, seqs),
        out_shape=jax.ShapeDtypeStruct((seqs, own + 16, HEAD), jnp.bfloat16),
        grid_spec=pltpu.PrefetchScalarGridSpec(
            num_scalar_prefetch=1,
            grid=(1,),
            in_specs=[
                pl.BlockSpec((requests, rows_each, HEAD), lambda i, t: (0, 0, 0)),
                pl.BlockSpec((limit,) + pool.shape[1:], lambda i, t: (0, 0, 0, 0)),
            ],
            out_specs=pl.BlockSpec((seqs, own + 16, HEAD), lambda i, t: (0, 0, 0)),
            scratch_shapes=[
                pltpu.VMEM((GROUPS * MEM * rows_each, HEAD), jnp.bfloat16),
                pltpu.VMEM((GROUPS * MEM * rows_each, HEAD), jnp.float32),
                pltpu.VMEM((GROUPS * MEM * rows_each // HEAD, HEAD), jnp.float32),
                pltpu.VMEM((HEAD, MEM * rows_each), jnp.float32),
            ],
        ),
        cost_estimate=pl.CostEstimate(
            flops=4 * limit * 64 * MEM * rows_each * HEAD,
            bytes_accessed=limit * 2 * 64 * HEAD * 2,
            transcendentals=limit * 64 * MEM * rows_each,
        ),
        name="attend",
    )(table, queries, pool)


def fresh_kernel(steps, q_ref, k_ref, v_ref, out_ref):
    rows = q_ref.shape[0]
    count = k_ref.shape[0] // steps
    rows_each = rows // count
    shape = (steps * count, rows)
    key = lax.broadcasted_iota(jnp.int32, shape, 0)
    lane = lax.broadcasted_iota(jnp.int32, shape, 1)
    seen = (lane // rows_each == lax.rem(key, count)) & (
        key // count <= lax.rem(lane, rows_each) // (rows_each // steps)
    )
    scores = lax.dot_general(
        k_ref[...], q_ref[...], (((1,), (1,)), ((), ())), preferred_element_type=jnp.float32
    ) * HEAD ** (-0.5)
    scores = jnp.where(seen, scores, NEG)
    peak = jnp.max(scores, 0, keepdims=True)
    expo = jnp.where(seen, jnp.exp(scores - peak), 0.0)
    total = jnp.sum(expo, 0, keepdims=True)
    value = lax.dot_general(
        v_ref[...],
        expo.astype(jnp.bfloat16),
        (((0,), (0,)), ((), ())),
        preferred_element_type=jnp.float32,
    )
    out_ref[pl.ds(0, rows), :] = (value * (1.0 / total)).T.astype(jnp.bfloat16)
    lse = peak + jnp.log(total)
    out_ref[pl.ds(rows, 16), :] = packed_tail(
        [lse[:, k * HEAD : (k + 1) * HEAD] for k in range(rows // HEAD)]
    )


def fresh_part(queries, keys, values, steps):
    rows = queries.shape[0]
    return pl.pallas_call(
        functools.partial(fresh_kernel, steps),
        out_shape=jax.ShapeDtypeStruct((rows + 16, HEAD), jnp.bfloat16),
        cost_estimate=pl.CostEstimate(
            flops=4 * rows * keys.shape[0] * HEAD, bytes_accessed=rows * HEAD * 4, transcendentals=0
        ),
        name="fresh",
    )(queries, keys, values)


def mix_refs(parts):
    rows = parts[0].shape[0] - 16
    blocks = rows // HEAD
    lses = []
    for part in parts:
        tail = part[pl.ds(rows, 16), :].astype(jnp.float32)
        lses.append(
            tail[0:blocks] + tail[blocks : 2 * blocks] + tail[2 * blocks : 3 * blocks]
        )
    peak = lses[0]
    for lse in lses[1:]:
        peak = jnp.maximum(peak, lse)
    fades = [jnp.exp(lse - peak) for lse in lses]
    total = sum(fades)
    inverse = 1.0 / total
    turned = [
        jnp.concatenate([fade * inverse, jnp.zeros((8 - blocks, HEAD), jnp.float32)], 0).T
        for fade in fades
    ]
    values = []
    for k in range(blocks):
        value = 0.0
        for part, weight in zip(parts, turned):
            value = value + part[pl.ds(k * HEAD, HEAD), :].astype(jnp.float32) * weight[:, k : k + 1]
        values.append(value)
    return values, peak + jnp.log(total)


def mix_kernel(*refs):
    out_ref = refs[-1]
    values, lse = mix_refs(refs[:-1])
    for k, value in enumerate(values):
        out_ref[pl.ds(k * HEAD, HEAD), :] = value.astype(jnp.bfloat16)
    out_ref[pl.ds(len(values) * HEAD, 16), :] = packed_tail(
        [lse[k : k + 1] for k in range(len(values))]
    )


def mix(parts):
    return pl.pallas_call(
        mix_kernel,
        out_shape=jax.ShapeDtypeStruct(parts[0].shape, jnp.bfloat16),
        cost_estimate=pl.CostEstimate(
            flops=2 * len(parts) * parts[0].size, bytes_accessed=parts[0].size * 10, transcendentals=0
        ),
        name="mix",
    )(*parts)


def final_kernel(ratio, *refs):
    parts, out_ref, scratch = refs[:-2], refs[-2], refs[-1]
    values, _ = mix_refs(parts)
    for k, value in enumerate(values):
        scratch[pl.ds(k * HEAD, HEAD), :] = value
    tokens = out_ref.shape[0]
    for h in range(ratio):
        out_ref[:, h * HEAD : (h + 1) * HEAD] = scratch[pl.ds(h, tokens, stride=ratio), :].astype(
            jnp.bfloat16
        )


def final(parts, ratio):
    rows = parts[0].shape[0] - 16
    return pl.pallas_call(
        functools.partial(final_kernel, ratio),
        out_shape=jax.ShapeDtypeStruct((rows // ratio, ratio * HEAD), jnp.bfloat16),
        scratch_shapes=[pltpu.VMEM((rows, HEAD), jnp.float32)],
        cost_estimate=pl.CostEstimate(
            flops=2 * len(parts) * parts[0].size, bytes_accessed=parts[0].size * 10, transcendentals=0
        ),
        name="final",
    )(*parts)


def page_table(owners, fills, group_of_request):
    requests = group_of_request.shape[0]
    count = owners.shape[0]
    index = jnp.arange(requests, dtype=jnp.int32)
    same = group_of_request[:, None] == group_of_request[None, :]
    rank = jnp.sum((same & (index[None, :] < index[:, None])).astype(jnp.int32), 1)
    slot = group_of_request * MEM + rank
    shared = owners >= requests
    own_slot = jnp.sum(jnp.where(owners[:, None] == index[None, :], slot[None, :], 0), 1)
    group = jnp.where(shared, owners - requests, own_slot // MEM)
    group = jnp.where(owners >= 0, group, GROUPS)
    code = jnp.where(shared, -1, own_slot % MEM)
    place = jnp.arange(count, dtype=jnp.int32)
    before = (group[None, :] < group[:, None]) | (
        (group[None, :] == group[:, None]) & (place[None, :] < place[:, None])
    )
    target = jnp.sum(before.astype(jnp.int32), 1)
    hit = target[None, :] == place[:, None]
    ordered = [
        jnp.sum(jnp.where(hit, row[None, :], 0), 1) for row in (place, fills, code)
    ]
    starts = jnp.sum(
        (group[None, :] < jnp.arange(8, dtype=jnp.int32)[:, None]).astype(jnp.int32), 1
    )
    return jnp.concatenate(ordered + [starts, slot])


CAP_SEQ = 44
CAP_ROW = 40


def earlier(count):
    index = jnp.arange(count, dtype=jnp.int32)
    return index[None, :] < index[:, None]


def counted(mask, axis):
    return jnp.sum(mask.astype(jnp.int32), axis)


def inverted(place, value, count):
    hit = place[None, :] == jnp.arange(count, dtype=jnp.int32)[:, None]
    return jnp.sum(jnp.where(hit, value[None, :], 0), 1)


def migration_tables(page_owner, migrate_dest, pool_size):
    rows, seqs = lax.axis_size("row"), lax.axis_size("seq")
    row, seq = lax.axis_index("row"), lax.axis_index("seq")
    limit = pool_size // 2
    cap = pool_size // (rows * seqs)
    dest = migrate_dest.reshape(rows, seqs, pool_size)[:, :, :limit]
    live = (page_owner >= 0).reshape(rows, seqs, pool_size)[:, :, :limit]
    dest = jnp.where(live, dest, -1)
    column = jnp.where(live, dest % seqs, -1)
    all_seq = jnp.arange(seqs, dtype=jnp.int32)
    in_column = counted(column[..., None, :] == all_seq[:, None], -1)
    everyone = jnp.arange(rows * seqs, dtype=jnp.int32)
    from_row = counted(dest.reshape(rows, 1, seqs * limit) == everyone[:, None], -1)
    fits = (jnp.max(in_column) <= CAP_SEQ) & (jnp.max(from_row) <= CAP_ROW)

    dest_row = lax.dynamic_index_in_dim(dest, row, 0, False)
    own = lax.dynamic_index_in_dim(dest_row, seq, 0, False)
    step = jnp.where(own >= 0, (own % seqs - seq + seqs) % seqs, -1)
    rank = counted((step[None, :] == step[:, None]) & earlier(limit), 1)
    place = jnp.where((step >= 0) & (rank < CAP_SEQ), step * CAP_SEQ + rank, -1)
    first = inverted(place, jnp.arange(limit, dtype=jnp.int32), seqs * CAP_SEQ)

    sender = (seq - all_seq + seqs) % seqs
    lists = jnp.sum(
        jnp.where((sender[:, None] == all_seq[None, :])[..., None], dest_row[None], 0), 1
    )
    lists = lists.reshape(seqs * limit)
    which = jnp.arange(seqs * limit, dtype=jnp.int32) // limit
    here = (lists >= 0) & (lists % seqs == seq)
    step = jnp.where(here, (lists // seqs - row + rows) % rows, -1)
    before = earlier(seqs * limit) & here[None, :]
    rank = counted(before & (which[None, :] == which[:, None]), 1)
    order = counted(before & (step[None, :] == step[:, None]), 1)
    place = jnp.where(here & (order < CAP_ROW), step * CAP_ROW + order, -1)
    second = inverted(place, which * CAP_SEQ + jnp.minimum(rank, CAP_SEQ - 1), rows * CAP_ROW)

    coming = counted(dest == row * seqs + seq, -1)
    ahead = (seq - all_seq + seqs) % seqs
    offset = jnp.sum(jnp.where(ahead[None, :] < ahead[:, None], coming[:, None, :], 0), -1)
    listed = (row - jnp.arange(rows, dtype=jnp.int32) + rows) % rows
    page = jnp.arange(cap, dtype=jnp.int32)
    third = (listed[:, None] * CAP_ROW + offset)[..., None] + page
    third = jnp.where(page < coming[..., None], jnp.minimum(third, rows * CAP_ROW - 1), -1)
    return fits, first, second, third.reshape(pool_size), coming.reshape(rows * seqs)


def split_kernel(table, pool_ref, *out_refs):
    lists = len(out_refs) // 2
    length = out_refs[0].shape[0]
    for k in range(lists):

        def move(i, _):
            page = table[k * length + i]
            out_refs[k][i] = pool_ref[page, 0]
            out_refs[lists + k][i] = pool_ref[page, 1]
            return 0

        lax.fori_loop(0, length, move, 0, unroll=4)


def split_pool(table, pool, lists):
    limit, _, page_len, width = (pool.shape[0] // 2,) + pool.shape[1:]
    length = table.shape[0] // lists
    shape = (length, page_len, width)
    return pl.pallas_call(
        split_kernel,
        out_shape=[jax.ShapeDtypeStruct(shape, pool.dtype)] * (2 * lists),
        grid_spec=pltpu.PrefetchScalarGridSpec(
            num_scalar_prefetch=1,
            grid=(1,),
            in_specs=[pl.BlockSpec((limit,) + pool.shape[1:], lambda i, t: (0, 0, 0, 0))],
            out_specs=[pl.BlockSpec(shape, lambda i, t: (0, 0, 0))] * (2 * lists),
        ),
        cost_estimate=pl.CostEstimate(
            flops=0, bytes_accessed=pool.size + 4 * lists * length * page_len * width, transcendentals=0
        ),
        name="split_pool",
    )(table, pool)


def resplit_kernel(count, table, *refs):
    sources, outs = refs[:count], refs[count : 2 * count]
    scratch, sems = refs[2 * count], refs[2 * count + 1]
    length = sources[0].shape[0]
    copies = [
        pltpu.make_async_copy(ref, scratch.at[pl.ds(k * length, length)], sems.at[k])
        for k, ref in enumerate(sources)
    ]
    for copy in copies:
        copy.start()
    for copy in copies:
        copy.wait()
    length_out = outs[0].shape[0]
    for k, out in enumerate(outs):

        def move(i, _):
            out[i] = scratch[table[k * length_out + i]]
            return 0

        lax.fori_loop(0, length_out, move, 0, unroll=4)


def resplit(table, lists):
    count = len(lists)
    length, page_len, width = lists[0].shape
    shape = (table.shape[0] // count, page_len, width)
    return pl.pallas_call(
        functools.partial(resplit_kernel, count),
        out_shape=[jax.ShapeDtypeStruct(shape, lists[0].dtype)] * count,
        grid_spec=pltpu.PrefetchScalarGridSpec(
            num_scalar_prefetch=1,
            grid=(1,),
            in_specs=[pl.BlockSpec(memory_space=pl.ANY)] * count,
            out_specs=[pl.BlockSpec(shape, lambda i, t: (0, 0, 0))] * count,
            scratch_shapes=[
                pltpu.VMEM((count * length, page_len, width), lists[0].dtype),
                pltpu.SemaphoreType.DMA((count,)),
            ],
        ),
        cost_estimate=pl.CostEstimate(
            flops=0, bytes_accessed=4 * count * length * page_len * width, transcendentals=0
        ),
        name="resplit",
    )(table, *lists)


def settle_kernel(count, table, *refs):
    sources, out, scratch, sems = refs[: 2 * count], refs[-3], refs[-2], refs[-1]
    length = sources[0].shape[0]
    block = out.shape[0]

    @pl.when(pl.program_id(0) == 0)
    def _():
        copies = [
            pltpu.make_async_copy(
                ref, scratch.at[k // count, pl.ds(k % count * length, length)], sems.at[k]
            )
            for k, ref in enumerate(sources)
        ]
        for copy in copies:
            copy.start()
        for copy in copies:
            copy.wait()

    for i in range(block):
        place = table[pl.program_id(0) * block + i]

        @pl.when(place >= 0)
        def _():
            for half in range(2):
                out[i, half] = scratch[half, place]

        @pl.when(place < 0)
        def _():
            out[i] = jnp.zeros(out.shape[1:], out.dtype)


def settle(table, keys, values, block):
    count = len(keys)
    length, page_len, width = keys[0].shape
    slots = table.shape[0]
    return pl.pallas_call(
        functools.partial(settle_kernel, count),
        out_shape=jax.ShapeDtypeStruct((slots, 2, page_len, width), keys[0].dtype),
        grid_spec=pltpu.PrefetchScalarGridSpec(
            num_scalar_prefetch=1,
            grid=(slots // block,),
            in_specs=[pl.BlockSpec(memory_space=pl.ANY)] * (2 * count),
            out_specs=pl.BlockSpec((block, 2, page_len, width), lambda i, t: (i, 0, 0, 0)),
            scratch_shapes=[
                pltpu.VMEM((2, count * length, page_len, width), keys[0].dtype),
                pltpu.SemaphoreType.DMA((2 * count,)),
            ],
        ),
        cost_estimate=pl.CostEstimate(
            flops=0, bytes_accessed=8 * slots * page_len * width, transcendentals=0
        ),
        name="settle",
    )(table, *keys, *values)


def passed(lists, axis):
    return [lists[0]] + [
        lax.ppermute(part, axis, ring(axis, k)) for k, part in enumerate(lists) if k
    ]


def rotate(values, cosine, sine):
    half = values.shape[-1] // 2
    first_half = values[..., :half]
    second_half = values[..., half:]
    return jnp.concatenate(
        [first_half * cosine - second_half * sine, second_half * cosine + first_half * sine], -1
    )


def migrate_whole(kv_pool, migrate_dest, coming, device):
    pool_size = kv_pool.shape[0]
    own_dest = lax.dynamic_slice_in_dim(migrate_dest, device * pool_size, pool_size)
    send_order = jnp.argsort(own_dest, stable=True)
    moved = lax.all_to_all(
        kv_pool[send_order], ("row", "seq"), split_axis=0, concat_axis=0, tiled=True
    )
    page = jnp.arange(pool_size // coming.shape[0], dtype=jnp.int32)
    full = (page[None, :] < coming[:, None]).reshape(pool_size)
    return jnp.where(full[:, None, None, None], moved, jnp.zeros_like(moved))


def block(
    hidden_in,
    norm_gain,
    w_qkv,
    w_out,
    kv_pool,
    page_owner,
    page_fill,
    lengths,
    group_of_request,
    migrate_dest,
):
    step_count, request_count, width_here = hidden_in.shape
    ratio = HEADS // KV_HEADS
    heads_here = w_qkv.shape[1] // ((ratio + 2) * HEAD)
    hidden_f = hidden_in.astype(jnp.float32)
    fits, first_table, second_table, third_table, coming = migration_tables(
        page_owner, migrate_dest, kv_pool.shape[0]
    )
    seqs = lax.axis_size("seq")
    lists = split_pool(first_table, kv_pool, seqs)
    key_lists = passed(lists[:seqs], "seq")
    value_lists = passed(lists[seqs:], "seq")
    row_start = lax.axis_index("row") * width_here
    gain_f = lax.dynamic_slice_in_dim(norm_gain, row_start, width_here).astype(jnp.float32)
    width = width_here * lax.axis_size("row")
    squares = jnp.sum(hidden_f * hidden_f, -1)
    partial_value = jnp.dot(
        (hidden_f * gain_f).astype(jnp.bfloat16).reshape(step_count * request_count, width_here),
        w_qkv,
        preferred_element_type=jnp.float32,
    ).astype(jnp.bfloat16)
    columns = partial_value.shape[1]
    extra = jnp.pad(jnp.stack(pieces(squares), -1), ((0, 0), (0, 0), (0, HEAD - 3)))
    partial_value = jnp.concatenate(
        [partial_value.reshape(step_count, request_count, columns), extra], 2
    )
    step_here = lax.axis_index("row")
    position = (lengths + step_here).astype(jnp.float32)
    half = HEAD // 2
    angle = position[:, None] * THETA ** (-(jnp.arange(half, dtype=jnp.float32) * 2.0 / HEAD))
    cosine, sine = lax.optimization_barrier((jnp.cos(angle), jnp.sin(angle)))
    summed = lax.dynamic_index_in_dim(partial_value, step_here, 0, False).astype(jnp.float32)
    arrived = exchanged(partial_value, "row")
    for part in arrived:
        summed = summed + part.astype(jnp.float32)
    scale = lax.rsqrt(jnp.sum(summed[:, columns : columns + 3], -1) / width + EPS)
    projected = (summed[:, :columns] * scale[:, None]).astype(jnp.bfloat16).astype(jnp.float32)
    projected = projected.reshape(request_count, heads_here * (ratio + 2), HEAD)
    rotated = rotate(projected, cosine[:, None], sine[:, None])
    is_value = jnp.arange(heads_here * (ratio + 2)) % (ratio + 2) == ratio + 1
    ready = jnp.where(is_value[None, :, None], projected, rotated).astype(jnp.bfloat16)
    ready = collected(ready, "row")
    ready = ready.reshape(step_count, request_count, heads_here, ratio + 2, HEAD)
    key_lists = resplit(second_table, key_lists)
    key_lists = passed(key_lists, "row")
    queries = ready[:, :, :, :ratio]
    keys_new = ready[:, :, :, ratio]
    values_new = ready[:, :, :, ratio + 1]
    local_req = request_count // lax.axis_size("seq")
    req_start = lax.axis_index("seq") * local_req
    new_kv = jnp.stack(
        [
            keys_new.reshape(step_count, request_count, heads_here * HEAD),
            values_new.reshape(step_count, request_count, heads_here * HEAD),
        ],
        2,
    )
    new_kv_local = lax.dynamic_slice_in_dim(new_kv, req_start, local_req, 1)
    device = lax.axis_index("row") * lax.axis_size("seq") + lax.axis_index("seq")
    pool_size = kv_pool.shape[0]
    owners_here = lax.dynamic_slice_in_dim(page_owner, device * pool_size, pool_size)
    fills = lax.dynamic_slice_in_dim(page_fill, device * pool_size, pool_size)
    live_limit = pool_size // 2
    table = page_table(owners_here[:live_limit], fills[:live_limit], group_of_request)
    rows_here = step_count * ratio
    rows_first = queries[:, :, 0].transpose(1, 0, 2, 3).reshape(request_count, rows_here, HEAD)
    seq_size = lax.axis_size("seq")
    own_rows = local_req * rows_here
    both = attend(table, rows_first, kv_pool, seq_size)
    parts = [lax.dynamic_index_in_dim(both, lax.axis_index("seq"), 0, False)]
    parts += exchanged(both, "seq")
    value_lists = resplit(second_table, value_lists)
    both = mix(parts)
    parts = [both] + [lax.ppermute(both, "row", ring("row", k)) for k in range(1, 4)]
    value_lists = passed(value_lists, "row")
    query_own = lax.dynamic_slice_in_dim(rows_first, req_start, local_req, 0)
    key_own = lax.dynamic_slice_in_dim(keys_new, req_start, local_req, 1)
    value_own = lax.dynamic_slice_in_dim(values_new, req_start, local_req, 1)
    own = fresh_part(
        query_own.reshape(own_rows, HEAD),
        key_own.reshape(step_count * local_req, HEAD),
        value_own.reshape(step_count * local_req, HEAD),
        step_count,
    )
    picked = final([own] + parts, ratio)
    partial_out = jnp.dot(picked, w_out, preferred_element_type=jnp.float32).astype(jnp.bfloat16)
    col_size = lax.axis_size("col")
    col_width = partial_out.shape[1] // col_size
    spread = partial_out.reshape(step_count * local_req, col_size, col_width).transpose(1, 0, 2)
    summed = jnp.sum(
        lax.all_to_all(spread, "col", 0, 0, tiled=True).astype(jnp.float32), 0
    )
    residual = lax.dynamic_slice_in_dim(
        lax.dynamic_slice_in_dim(hidden_f, req_start, local_req, 1),
        lax.axis_index("col") * col_width,
        col_width,
        2,
    )
    summed = summed.reshape(local_req, step_count, col_width).transpose(1, 0, 2)
    layer_out = (summed + residual).astype(jnp.bfloat16)
    moved = lax.cond(
        fits,
        lambda: settle(third_table, key_lists, value_lists, kv_pool.shape[0] // coming.shape[0]),
        lambda: migrate_whole(kv_pool, migrate_dest, coming, device),
    )
    return (layer_out, new_kv_local, moved)


def solution(mesh):
    in_specs = (
        P(None, None, "row"),
        P(),
        P("row", "col"),
        P("col", "row"),
        P(("row", "seq"), None, None, "col"),
        P(),
        P(),
        P(),
        P(),
        P(),
    )
    out_specs = (
        P(None, "seq", ("row", "col")),
        P(None, "seq", None, "col"),
        P(("row", "seq"), None, None, "col"),
    )
    return jax.shard_map(block, mesh=mesh, in_specs=in_specs, out_specs=out_specs, check_vma=False)
```

```python
import functools
import math

import jax
import jax.numpy as jnp
from jax import lax
from jax.experimental import pallas as pl
from jax.experimental.pallas import tpu as pltpu
from jax.sharding import PartitionSpec as P

HEADS = 64
KV_HEADS = 8
HEAD = 128
GROUPS = 4
MEM = 16


EPS = 1e-06
THETA = 1000000.0
NEG = -1e30


def ring(axis, step):
    size = lax.axis_size(axis)
    return [(k, (k + step) % size) for k in range(size)]


def exchanged(parts, axis):
    size = lax.axis_size(axis)
    here = lax.axis_index(axis)
    return [
        lax.ppermute(
            lax.dynamic_index_in_dim(parts, (here + step) % size, 0, False), axis, ring(axis, step)
        )
        for step in range(1, size)
    ]


def collected(part, axis):
    size = lax.axis_size(axis)
    here = lax.axis_index(axis)
    ahead = [part] + [lax.ppermute(part, axis, ring(axis, size - step)) for step in range(1, size)]
    twice = jnp.stack(ahead + ahead[:-1])
    return lax.dynamic_slice_in_dim(twice, (size - here) % size, size, 0)


def pieces(value):
    high = lax.reduce_precision(value, 8, 7)
    middle = lax.reduce_precision(value - high, 8, 7)
    low = value - high - middle
    return [high.astype(jnp.bfloat16), middle.astype(jnp.bfloat16), low.astype(jnp.bfloat16)]


def packed_tail(lse_rows):
    count = len(lse_rows)
    row = lax.broadcasted_iota(jnp.int32, (16, HEAD), 0)
    tail = jnp.zeros((16, HEAD), jnp.float32)
    for index, lse in enumerate(lse_rows):
        high = lse.astype(jnp.bfloat16).astype(jnp.float32)
        middle = (lse - high).astype(jnp.bfloat16).astype(jnp.float32)
        low = lse - high - middle
        for k, term in enumerate((high, middle, low)):
            tail = jnp.where(row == k * count + index, jnp.broadcast_to(term, (16, HEAD)), tail)
    return tail.astype(jnp.bfloat16)


def attend_kernel(seqs, table, q_ref, pool_ref, out_ref, grouped, gathered, lse_rows, acc):
    page_len = pool_ref.shape[2]
    limit = pool_ref.shape[0]
    rows_each = q_ref.shape[1]
    requests = q_ref.shape[0]
    row_count = MEM * rows_each
    at_fill, at_code, at_start, at_slot = limit, 2 * limit, 3 * limit, 3 * limit + 8
    factor = HEAD ** (-0.5) * math.log2(math.e)
    grouped[...] = jnp.zeros_like(grouped)
    for r in range(requests):
        slot = table[at_slot + r]
        grouped[pl.ds(pl.multiple_of(slot * rows_each, rows_each), rows_each), :] = q_ref[r]
    lane_slot = lax.broadcasted_iota(jnp.int32, (1, row_count), 1) // rows_each
    token = lax.broadcasted_iota(jnp.int32, (page_len, row_count), 0)
    for g in range(GROUPS):
        first = table[at_start + g]
        last = table[at_start + g + 1]
        acc[...] = jnp.zeros_like(acc)

        def visit(number, carry):
            old_max, old_sum = carry
            base = first + number * TILE
            places = [jnp.minimum(base + i, limit - 1) for i in range(TILE)]
            keys = jnp.concatenate([pool_ref[table[p], 0] for p in places], 0)
            values = jnp.concatenate([pool_ref[table[p], 1] for p in places], 0)
            scores = lax.dot_general(
                keys,
                grouped[pl.ds(g * row_count, row_count), :],
                (((1,), (1,)), ((), ())),
                preferred_element_type=jnp.float32,
            )
            shown = []
            for i, p in enumerate(places):
                fill = jnp.where(base + i < last, table[at_fill + p], 0)
                code = table[at_code + p]
                rows_ok = jnp.where((lane_slot == code) | (code < 0), fill, 0)
                part = scores[i * page_len : (i + 1) * page_len]
                shown.append(jnp.where(token < rows_ok, part, NEG))
            new_max = old_max
            for part in shown:
                new_max = jnp.maximum(new_max, jnp.max(part, 0, keepdims=True))
            base_max = jnp.where(new_max > 0.5 * NEG, new_max, 0.0)
            fade = jnp.exp2((old_max - base_max) * factor)
            expo = [jnp.exp2((part - base_max) * factor) for part in shown]
            new_sum = old_sum * fade
            for part in expo:
                new_sum = new_sum + jnp.sum(part, 0, keepdims=True)
            weights = jnp.concatenate([part.astype(jnp.bfloat16) for part in expo], 0)
            acc[...] = acc[...] * fade + lax.dot_general(
                values, weights, (((0,), (0,)), ((), ())), preferred_element_type=jnp.float32
            )
            return new_max, new_sum

        start = (
            jnp.full((1, row_count), NEG, jnp.float32),
            jnp.zeros((1, row_count), jnp.float32),
        )
        run_max, run_sum = lax.fori_loop(0, (last - first + TILE - 1) // TILE, visit, start)
        held = run_sum > 0
        safe = jnp.where(held, run_sum, 1.0)
        lse = jnp.where(held, run_max * HEAD ** (-0.5) + jnp.log(safe), NEG)
        gathered[pl.ds(g * row_count, row_count), :] = (acc[...] * (1.0 / safe)).T
        for k in range(row_count // HEAD):
            lse_rows[pl.ds(g * (row_count // HEAD) + k, 1), :] = lse[:, k * HEAD : (k + 1) * HEAD]
    lane = lax.broadcasted_iota(jnp.int32, (8, HEAD), 1) // rows_each
    each = requests // seqs
    per_row = HEAD // rows_each
    for s in range(seqs):
        tails = []
        for k in range(each // per_row):
            line = jnp.zeros((8, HEAD), jnp.float32)
            for i in range(per_row):
                r = s * each + k * per_row + i
                slot = table[at_slot + r]
                out_ref[s, pl.ds((k * per_row + i) * rows_each, rows_each), :] = gathered[
                    pl.ds(pl.multiple_of(slot * rows_each, rows_each), rows_each), :
                ].astype(jnp.bfloat16)
                source = jnp.broadcast_to(lse_rows[pl.ds(slot // per_row, 1), :], (8, HEAD))
                shift = lax.rem(i - lax.rem(slot, per_row) + per_row, per_row) * rows_each
                line = jnp.where(lane == i, pltpu.roll(source, shift, 1), line)
            tails.append(line[0:1])
        out_ref[s, pl.ds(each * rows_each, 16), :] = packed_tail(tails)


TILE = 8


def attend(table, queries, pool, seqs):
    requests, rows_each, _ = queries.shape
    limit = pool.shape[0] // 2
    own = requests // seqs * rows_each
    return pl.pallas_call(
        functools.partial(attend_kernel, seqs),
        out_shape=jax.ShapeDtypeStruct((seqs, own + 16, HEAD), jnp.bfloat16),
        grid_spec=pltpu.PrefetchScalarGridSpec(
            num_scalar_prefetch=1,
            grid=(1,),
            in_specs=[
                pl.BlockSpec((requests, rows_each, HEAD), lambda i, t: (0, 0, 0)),
                pl.BlockSpec((limit,) + pool.shape[1:], lambda i, t: (0, 0, 0, 0)),
            ],
            out_specs=pl.BlockSpec((seqs, own + 16, HEAD), lambda i, t: (0, 0, 0)),
            scratch_shapes=[
                pltpu.VMEM((GROUPS * MEM * rows_each, HEAD), jnp.bfloat16),
                pltpu.VMEM((GROUPS * MEM * rows_each, HEAD), jnp.float32),
                pltpu.VMEM((GROUPS * MEM * rows_each // HEAD, HEAD), jnp.float32),
                pltpu.VMEM((HEAD, MEM * rows_each), jnp.float32),
            ],
        ),
        cost_estimate=pl.CostEstimate(
            flops=4 * limit * 64 * MEM * rows_each * HEAD,
            bytes_accessed=limit * 2 * 64 * HEAD * 2,
            transcendentals=limit * 64 * MEM * rows_each,
        ),
        name="attend",
    )(table, queries, pool)


def fresh_kernel(steps, q_ref, k_ref, v_ref, out_ref):
    rows = q_ref.shape[0]
    count = k_ref.shape[0] // steps
    rows_each = rows // count
    shape = (steps * count, rows)
    key = lax.broadcasted_iota(jnp.int32, shape, 0)
    lane = lax.broadcasted_iota(jnp.int32, shape, 1)
    seen = (lane // rows_each == lax.rem(key, count)) & (
        key // count <= lax.rem(lane, rows_each) // (rows_each // steps)
    )
    scores = lax.dot_general(
        k_ref[...], q_ref[...], (((1,), (1,)), ((), ())), preferred_element_type=jnp.float32
    ) * HEAD ** (-0.5)
    scores = jnp.where(seen, scores, NEG)
    peak = jnp.max(scores, 0, keepdims=True)
    expo = jnp.where(seen, jnp.exp(scores - peak), 0.0)
    total = jnp.sum(expo, 0, keepdims=True)
    value = lax.dot_general(
        v_ref[...],
        expo.astype(jnp.bfloat16),
        (((0,), (0,)), ((), ())),
        preferred_element_type=jnp.float32,
    )
    out_ref[pl.ds(0, rows), :] = (value * (1.0 / total)).T.astype(jnp.bfloat16)
    lse = peak + jnp.log(total)
    out_ref[pl.ds(rows, 16), :] = packed_tail(
        [lse[:, k * HEAD : (k + 1) * HEAD] for k in range(rows // HEAD)]
    )


def fresh_part(queries, keys, values, steps):
    rows = queries.shape[0]
    return pl.pallas_call(
        functools.partial(fresh_kernel, steps),
        out_shape=jax.ShapeDtypeStruct((rows + 16, HEAD), jnp.bfloat16),
        cost_estimate=pl.CostEstimate(
            flops=4 * rows * keys.shape[0] * HEAD, bytes_accessed=rows * HEAD * 4, transcendentals=0
        ),
        name="fresh",
    )(queries, keys, values)


def mix_refs(parts):
    rows = parts[0].shape[0] - 16
    blocks = rows // HEAD
    lses = []
    for part in parts:
        tail = part[pl.ds(rows, 16), :].astype(jnp.float32)
        lses.append(
            tail[0:blocks] + tail[blocks : 2 * blocks] + tail[2 * blocks : 3 * blocks]
        )
    peak = lses[0]
    for lse in lses[1:]:
        peak = jnp.maximum(peak, lse)
    fades = [jnp.exp(lse - peak) for lse in lses]
    total = sum(fades)
    inverse = 1.0 / total
    turned = [
        jnp.concatenate([fade * inverse, jnp.zeros((8 - blocks, HEAD), jnp.float32)], 0).T
        for fade in fades
    ]
    values = []
    for k in range(blocks):
        value = 0.0
        for part, weight in zip(parts, turned):
            value = value + part[pl.ds(k * HEAD, HEAD), :].astype(jnp.float32) * weight[:, k : k + 1]
        values.append(value)
    return values, peak + jnp.log(total)


def mix_kernel(*refs):
    out_ref = refs[-1]
    values, lse = mix_refs(refs[:-1])
    for k, value in enumerate(values):
        out_ref[pl.ds(k * HEAD, HEAD), :] = value.astype(jnp.bfloat16)
    out_ref[pl.ds(len(values) * HEAD, 16), :] = packed_tail(
        [lse[k : k + 1] for k in range(len(values))]
    )


def mix(parts):
    return pl.pallas_call(
        mix_kernel,
        out_shape=jax.ShapeDtypeStruct(parts[0].shape, jnp.bfloat16),
        cost_estimate=pl.CostEstimate(
            flops=2 * len(parts) * parts[0].size, bytes_accessed=parts[0].size * 10, transcendentals=0
        ),
        name="mix",
    )(*parts)


def final_kernel(ratio, *refs):
    parts, out_ref, scratch = refs[:-2], refs[-2], refs[-1]
    values, _ = mix_refs(parts)
    for k, value in enumerate(values):
        scratch[pl.ds(k * HEAD, HEAD), :] = value
    tokens = out_ref.shape[0]
    for h in range(ratio):
        out_ref[:, h * HEAD : (h + 1) * HEAD] = scratch[pl.ds(h, tokens, stride=ratio), :].astype(
            jnp.bfloat16
        )


def final(parts, ratio):
    rows = parts[0].shape[0] - 16
    return pl.pallas_call(
        functools.partial(final_kernel, ratio),
        out_shape=jax.ShapeDtypeStruct((rows // ratio, ratio * HEAD), jnp.bfloat16),
        scratch_shapes=[pltpu.VMEM((rows, HEAD), jnp.float32)],
        cost_estimate=pl.CostEstimate(
            flops=2 * len(parts) * parts[0].size, bytes_accessed=parts[0].size * 10, transcendentals=0
        ),
        name="final",
    )(*parts)


def page_table(owners, fills, group_of_request):
    requests = group_of_request.shape[0]
    count = owners.shape[0]
    index = jnp.arange(requests, dtype=jnp.int32)
    same = group_of_request[:, None] == group_of_request[None, :]
    rank = jnp.sum((same & (index[None, :] < index[:, None])).astype(jnp.int32), 1)
    slot = group_of_request * MEM + rank
    shared = owners >= requests
    own_slot = jnp.sum(jnp.where(owners[:, None] == index[None, :], slot[None, :], 0), 1)
    group = jnp.where(shared, owners - requests, own_slot // MEM)
    group = jnp.where(owners >= 0, group, GROUPS)
    code = jnp.where(shared, -1, own_slot % MEM)
    place = jnp.arange(count, dtype=jnp.int32)
    before = (group[None, :] < group[:, None]) | (
        (group[None, :] == group[:, None]) & (place[None, :] < place[:, None])
    )
    target = jnp.sum(before.astype(jnp.int32), 1)
    hit = target[None, :] == place[:, None]
    ordered = [
        jnp.sum(jnp.where(hit, row[None, :], 0), 1) for row in (place, fills, code)
    ]
    starts = jnp.sum(
        (group[None, :] < jnp.arange(8, dtype=jnp.int32)[:, None]).astype(jnp.int32), 1
    )
    return jnp.concatenate(ordered + [starts, slot])


CAP_SEQ = 44
CAP_ROW = 40


def earlier(count):
    index = jnp.arange(count, dtype=jnp.int32)
    return index[None, :] < index[:, None]


def counted(mask, axis):
    return jnp.sum(mask.astype(jnp.int32), axis)


def inverted(place, value, count):
    hit = place[None, :] == jnp.arange(count, dtype=jnp.int32)[:, None]
    return jnp.sum(jnp.where(hit, value[None, :], 0), 1)


def migration_tables(page_owner, migrate_dest, pool_size):
    rows, seqs = lax.axis_size("row"), lax.axis_size("seq")
    row, seq = lax.axis_index("row"), lax.axis_index("seq")
    limit = pool_size // 2
    cap = pool_size // (rows * seqs)
    dest = migrate_dest.reshape(rows, seqs, pool_size)[:, :, :limit]
    live = (page_owner >= 0).reshape(rows, seqs, pool_size)[:, :, :limit]
    dest = jnp.where(live, dest, -1)
    column = jnp.where(live, dest % seqs, -1)
    all_seq = jnp.arange(seqs, dtype=jnp.int32)
    in_column = counted(column[..., None, :] == all_seq[:, None], -1)
    everyone = jnp.arange(rows * seqs, dtype=jnp.int32)
    from_row = counted(dest.reshape(rows, 1, seqs * limit) == everyone[:, None], -1)
    fits = (jnp.max(in_column) <= CAP_SEQ) & (jnp.max(from_row) <= CAP_ROW)

    dest_row = lax.dynamic_index_in_dim(dest, row, 0, False)
    own = lax.dynamic_index_in_dim(dest_row, seq, 0, False)
    step = jnp.where(own >= 0, (own % seqs - seq + seqs) % seqs, -1)
    rank = counted((step[None, :] == step[:, None]) & earlier(limit), 1)
    place = jnp.where((step >= 0) & (rank < CAP_SEQ), step * CAP_SEQ + rank, -1)
    first = inverted(place, jnp.arange(limit, dtype=jnp.int32), seqs * CAP_SEQ)

    sender = (seq - all_seq + seqs) % seqs
    lists = jnp.sum(
        jnp.where((sender[:, None] == all_seq[None, :])[..., None], dest_row[None], 0), 1
    )
    lists = lists.reshape(seqs * limit)
    which = jnp.arange(seqs * limit, dtype=jnp.int32) // limit
    here = (lists >= 0) & (lists % seqs == seq)
    step = jnp.where(here, (lists // seqs - row + rows) % rows, -1)
    before = earlier(seqs * limit) & here[None, :]
    rank = counted(before & (which[None, :] == which[:, None]), 1)
    order = counted(before & (step[None, :] == step[:, None]), 1)
    place = jnp.where(here & (order < CAP_ROW), step * CAP_ROW + order, -1)
    second = inverted(place, which * CAP_SEQ + jnp.minimum(rank, CAP_SEQ - 1), rows * CAP_ROW)

    coming = counted(dest == row * seqs + seq, -1)
    ahead = (seq - all_seq + seqs) % seqs
    offset = jnp.sum(jnp.where(ahead[None, :] < ahead[:, None], coming[:, None, :], 0), -1)
    listed = (row - jnp.arange(rows, dtype=jnp.int32) + rows) % rows
    page = jnp.arange(cap, dtype=jnp.int32)
    third = (listed[:, None] * CAP_ROW + offset)[..., None] + page
    third = jnp.where(page < coming[..., None], jnp.minimum(third, rows * CAP_ROW - 1), -1)
    return fits, first, second, third.reshape(pool_size), coming.reshape(rows * seqs)


def split_kernel(table, pool_ref, *refs):
    out_refs, scratch, arrived, sems = refs[:-3], refs[-3], refs[-2], refs[-1]
    lists = len(out_refs) // 2
    length = out_refs[0].shape[0]
    copy = pltpu.make_async_copy(pool_ref.at[pl.ds(0, scratch.shape[0])], scratch, arrived)
    copy.start()
    copy.wait()
    for k in range(lists):

        def move(i, _):
            page = table[k * length + i]
            for half in range(2):
                pltpu.make_async_copy(
                    scratch.at[page, half], out_refs[half * lists + k].at[i], sems.at[half * lists + k]
                ).start()
            return 0

        lax.fori_loop(0, length, move, 0, unroll=4)
    for k, out in enumerate(out_refs):
        pltpu.make_async_copy(out, out, sems.at[k]).wait()


def split_pool(table, pool, lists):
    limit, _, page_len, width = (pool.shape[0] // 2,) + pool.shape[1:]
    length = table.shape[0] // lists
    shape = (length, page_len, width)
    return pl.pallas_call(
        split_kernel,
        out_shape=[jax.ShapeDtypeStruct(shape, pool.dtype)] * (2 * lists),
        grid_spec=pltpu.PrefetchScalarGridSpec(
            num_scalar_prefetch=1,
            grid=(1,),
            in_specs=[pl.BlockSpec(memory_space=pl.ANY)],
            out_specs=[pl.BlockSpec(memory_space=pl.ANY)] * (2 * lists),
            scratch_shapes=[
                pltpu.VMEM((limit,) + pool.shape[1:], pool.dtype),
                pltpu.SemaphoreType.DMA,
                pltpu.SemaphoreType.DMA((2 * lists,)),
            ],
        ),
        cost_estimate=pl.CostEstimate(
            flops=0, bytes_accessed=pool.size + 4 * lists * length * page_len * width, transcendentals=0
        ),
        name="split_pool",
    )(table, pool)


def resplit_kernel(count, table, *refs):
    sources, outs = refs[:count], refs[count : 2 * count]
    scratch, arrived, sems = refs[2 * count :]
    length = sources[0].shape[0]
    copies = [
        pltpu.make_async_copy(ref, scratch.at[pl.ds(k * length, length)], arrived.at[k])
        for k, ref in enumerate(sources)
    ]
    for copy in copies:
        copy.start()
    for copy in copies:
        copy.wait()
    length_out = outs[0].shape[0]
    for k, out in enumerate(outs):

        def move(i, _):
            pltpu.make_async_copy(
                scratch.at[table[k * length_out + i]], out.at[i], sems.at[k]
            ).start()
            return 0

        lax.fori_loop(0, length_out, move, 0, unroll=4)
    for k, out in enumerate(outs):
        pltpu.make_async_copy(out, out, sems.at[k]).wait()


def resplit(table, lists):
    count = len(lists)
    length, page_len, width = lists[0].shape
    shape = (table.shape[0] // count, page_len, width)
    return pl.pallas_call(
        functools.partial(resplit_kernel, count),
        out_shape=[jax.ShapeDtypeStruct(shape, lists[0].dtype)] * count,
        grid_spec=pltpu.PrefetchScalarGridSpec(
            num_scalar_prefetch=1,
            grid=(1,),
            in_specs=[pl.BlockSpec(memory_space=pl.ANY)] * count,
            out_specs=[pl.BlockSpec(memory_space=pl.ANY)] * count,
            scratch_shapes=[
                pltpu.VMEM((count * length, page_len, width), lists[0].dtype),
                pltpu.SemaphoreType.DMA((count,)),
                pltpu.SemaphoreType.DMA((count,)),
            ],
        ),
        cost_estimate=pl.CostEstimate(
            flops=0, bytes_accessed=4 * count * length * page_len * width, transcendentals=0
        ),
        name="resplit",
    )(table, *lists)


def settle_kernel(count, table, *refs):
    sources, out, scratch, zero, sems, done = refs[: 2 * count], refs[-5], refs[-4], refs[-3], refs[-2], refs[-1]
    length = sources[0].shape[0]
    copies = [
        pltpu.make_async_copy(
            ref, scratch.at[k // count, pl.ds(k % count * length, length)], sems.at[k]
        )
        for k, ref in enumerate(sources)
    ]
    for copy in copies:
        copy.start()
    zero[...] = jnp.zeros_like(zero)
    for copy in copies:
        copy.wait()

    def place_page(i, _):
        place = table[i]

        @pl.when(place >= 0)
        def _():
            for half in range(2):
                pltpu.make_async_copy(scratch.at[half, place], out.at[i, half], done).start()

        @pl.when(place < 0)
        def _():
            pltpu.make_async_copy(zero, out.at[i], done).start()

        return 0

    lax.fori_loop(0, out.shape[0], place_page, 0, unroll=4)
    pltpu.make_async_copy(out, out, done).wait()


def settle(table, keys, values):
    count = len(keys)
    length, page_len, width = keys[0].shape
    slots = table.shape[0]
    kind = keys[0].dtype
    return pl.pallas_call(
        functools.partial(settle_kernel, count),
        out_shape=jax.ShapeDtypeStruct((slots, 2, page_len, width), kind),
        grid_spec=pltpu.PrefetchScalarGridSpec(
            num_scalar_prefetch=1,
            grid=(1,),
            in_specs=[pl.BlockSpec(memory_space=pl.ANY)] * (2 * count),
            out_specs=pl.BlockSpec(memory_space=pl.ANY),
            scratch_shapes=[
                pltpu.VMEM((2, count * length, page_len, width), kind),
                pltpu.VMEM((2, page_len, width), kind),
                pltpu.SemaphoreType.DMA((2 * count,)),
                pltpu.SemaphoreType.DMA,
            ],
        ),
        cost_estimate=pl.CostEstimate(
            flops=0, bytes_accessed=8 * slots * page_len * width, transcendentals=0
        ),
        name="settle",
    )(table, *keys, *values)


def passed(lists, axis):
    return [lists[0]] + [
        lax.ppermute(part, axis, ring(axis, k)) for k, part in enumerate(lists) if k
    ]


def rotate(values, cosine, sine):
    half = values.shape[-1] // 2
    first_half = values[..., :half]
    second_half = values[..., half:]
    return jnp.concatenate(
        [first_half * cosine - second_half * sine, second_half * cosine + first_half * sine], -1
    )


def migrate_whole(kv_pool, migrate_dest, coming, device):
    pool_size = kv_pool.shape[0]
    own_dest = lax.dynamic_slice_in_dim(migrate_dest, device * pool_size, pool_size)
    send_order = jnp.argsort(own_dest, stable=True)
    moved = lax.all_to_all(
        kv_pool[send_order], ("row", "seq"), split_axis=0, concat_axis=0, tiled=True
    )
    page = jnp.arange(pool_size // coming.shape[0], dtype=jnp.int32)
    full = (page[None, :] < coming[:, None]).reshape(pool_size)
    return jnp.where(full[:, None, None, None], moved, jnp.zeros_like(moved))


def block(
    hidden_in,
    norm_gain,
    w_qkv,
    w_out,
    kv_pool,
    page_owner,
    page_fill,
    lengths,
    group_of_request,
    migrate_dest,
):
    step_count, request_count, width_here = hidden_in.shape
    ratio = HEADS // KV_HEADS
    heads_here = w_qkv.shape[1] // ((ratio + 2) * HEAD)
    hidden_f = hidden_in.astype(jnp.float32)
    fits, first_table, second_table, third_table, coming = migration_tables(
        page_owner, migrate_dest, kv_pool.shape[0]
    )
    seqs = lax.axis_size("seq")
    lists = split_pool(first_table, kv_pool, seqs)
    key_lists = passed(lists[:seqs], "seq")
    value_lists = passed(lists[seqs:], "seq")
    row_start = lax.axis_index("row") * width_here
    gain_f = lax.dynamic_slice_in_dim(norm_gain, row_start, width_here).astype(jnp.float32)
    width = width_here * lax.axis_size("row")
    squares = jnp.sum(hidden_f * hidden_f, -1)
    partial_value = jnp.dot(
        (hidden_f * gain_f).astype(jnp.bfloat16).reshape(step_count * request_count, width_here),
        w_qkv,
        preferred_element_type=jnp.float32,
    ).astype(jnp.bfloat16)
    columns = partial_value.shape[1]
    extra = jnp.pad(jnp.stack(pieces(squares), -1), ((0, 0), (0, 0), (0, HEAD - 3)))
    partial_value = jnp.concatenate(
        [partial_value.reshape(step_count, request_count, columns), extra], 2
    )
    step_here = lax.axis_index("row")
    position = (lengths + step_here).astype(jnp.float32)
    half = HEAD // 2
    angle = position[:, None] * THETA ** (-(jnp.arange(half, dtype=jnp.float32) * 2.0 / HEAD))
    cosine, sine = lax.optimization_barrier((jnp.cos(angle), jnp.sin(angle)))
    summed = lax.dynamic_index_in_dim(partial_value, step_here, 0, False).astype(jnp.float32)
    arrived = exchanged(partial_value, "row")
    for part in arrived:
        summed = summed + part.astype(jnp.float32)
    scale = lax.rsqrt(jnp.sum(summed[:, columns : columns + 3], -1) / width + EPS)
    projected = (summed[:, :columns] * scale[:, None]).astype(jnp.bfloat16).astype(jnp.float32)
    projected = projected.reshape(request_count, heads_here * (ratio + 2), HEAD)
    rotated = rotate(projected, cosine[:, None], sine[:, None])
    is_value = jnp.arange(heads_here * (ratio + 2)) % (ratio + 2) == ratio + 1
    ready = jnp.where(is_value[None, :, None], projected, rotated).astype(jnp.bfloat16)
    ready = collected(ready, "row")
    ready = ready.reshape(step_count, request_count, heads_here, ratio + 2, HEAD)
    key_lists = resplit(second_table, key_lists)
    key_lists = passed(key_lists, "row")
    queries = ready[:, :, :, :ratio]
    keys_new = ready[:, :, :, ratio]
    values_new = ready[:, :, :, ratio + 1]
    local_req = request_count // lax.axis_size("seq")
    req_start = lax.axis_index("seq") * local_req
    new_kv = jnp.stack(
        [
            keys_new.reshape(step_count, request_count, heads_here * HEAD),
            values_new.reshape(step_count, request_count, heads_here * HEAD),
        ],
        2,
    )
    new_kv_local = lax.dynamic_slice_in_dim(new_kv, req_start, local_req, 1)
    device = lax.axis_index("row") * lax.axis_size("seq") + lax.axis_index("seq")
    pool_size = kv_pool.shape[0]
    owners_here = lax.dynamic_slice_in_dim(page_owner, device * pool_size, pool_size)
    fills = lax.dynamic_slice_in_dim(page_fill, device * pool_size, pool_size)
    live_limit = pool_size // 2
    table = page_table(owners_here[:live_limit], fills[:live_limit], group_of_request)
    rows_here = step_count * ratio
    rows_first = queries[:, :, 0].transpose(1, 0, 2, 3).reshape(request_count, rows_here, HEAD)
    seq_size = lax.axis_size("seq")
    own_rows = local_req * rows_here
    both = attend(table, rows_first, kv_pool, seq_size)
    parts = [lax.dynamic_index_in_dim(both, lax.axis_index("seq"), 0, False)]
    parts += exchanged(both, "seq")
    query_own = lax.dynamic_slice_in_dim(rows_first, req_start, local_req, 0)
    key_own = lax.dynamic_slice_in_dim(keys_new, req_start, local_req, 1)
    value_own = lax.dynamic_slice_in_dim(values_new, req_start, local_req, 1)
    own = fresh_part(
        query_own.reshape(own_rows, HEAD),
        key_own.reshape(step_count * local_req, HEAD),
        value_own.reshape(step_count * local_req, HEAD),
        step_count,
    )
    value_lists = resplit(second_table, value_lists)
    both = mix(parts)
    parts = [both] + [lax.ppermute(both, "row", ring("row", k)) for k in range(1, 4)]
    value_lists = passed(value_lists, "row")
    picked = final([own] + parts, ratio)
    partial_out = jnp.dot(picked, w_out, preferred_element_type=jnp.float32).astype(jnp.bfloat16)
    col_size = lax.axis_size("col")
    col_width = partial_out.shape[1] // col_size
    spread = partial_out.reshape(step_count * local_req, col_size, col_width).transpose(1, 0, 2)
    summed = jnp.sum(
        lax.all_to_all(spread, "col", 0, 0, tiled=True).astype(jnp.float32), 0
    )
    residual = lax.dynamic_slice_in_dim(
        lax.dynamic_slice_in_dim(hidden_f, req_start, local_req, 1),
        lax.axis_index("col") * col_width,
        col_width,
        2,
    )
    summed = summed.reshape(local_req, step_count, col_width).transpose(1, 0, 2)
    layer_out = (summed + residual).astype(jnp.bfloat16)
    moved = lax.cond(
        fits,
        lambda: settle(third_table, key_lists, value_lists),
        lambda: migrate_whole(kv_pool, migrate_dest, coming, device),
    )
    return (layer_out, new_kv_local, moved)


def solution(mesh):
    in_specs = (
        P(None, None, "row"),
        P(),
        P("row", "col"),
        P("col", "row"),
        P(("row", "seq"), None, None, "col"),
        P(),
        P(),
        P(),
        P(),
        P(),
    )
    out_specs = (
        P(None, "seq", ("row", "col")),
        P(None, "seq", None, "col"),
        P(("row", "seq"), None, None, "col"),
    )
    return jax.shard_map(block, mesh=mesh, in_specs=in_specs, out_specs=out_specs, check_vma=False)
```

```python
import functools
import math

import jax
import jax.numpy as jnp
from jax import lax
from jax.experimental import pallas as pl
from jax.experimental.pallas import tpu as pltpu
from jax.sharding import PartitionSpec as P

HEADS = 64
KV_HEADS = 8
HEAD = 128
GROUPS = 4
MEM = 16


EPS = 1e-06
THETA = 1000000.0
NEG = -1e30


def ring(axis, step):
    size = lax.axis_size(axis)
    return [(k, (k + step) % size) for k in range(size)]


def exchanged(parts, axis):
    size = lax.axis_size(axis)
    here = lax.axis_index(axis)
    return [
        lax.ppermute(
            lax.dynamic_index_in_dim(parts, (here + step) % size, 0, False), axis, ring(axis, step)
        )
        for step in range(1, size)
    ]


def collected(part, axis):
    size = lax.axis_size(axis)
    here = lax.axis_index(axis)
    ahead = [part] + [lax.ppermute(part, axis, ring(axis, size - step)) for step in range(1, size)]
    twice = jnp.stack(ahead + ahead[:-1])
    return lax.dynamic_slice_in_dim(twice, (size - here) % size, size, 0)


def pieces(value):
    high = lax.reduce_precision(value, 8, 7)
    middle = lax.reduce_precision(value - high, 8, 7)
    low = value - high - middle
    return [high.astype(jnp.bfloat16), middle.astype(jnp.bfloat16), low.astype(jnp.bfloat16)]


def packed_tail(lse_rows):
    count = len(lse_rows)
    row = lax.broadcasted_iota(jnp.int32, (16, HEAD), 0)
    tail = jnp.zeros((16, HEAD), jnp.float32)
    for index, lse in enumerate(lse_rows):
        high = lse.astype(jnp.bfloat16).astype(jnp.float32)
        middle = (lse - high).astype(jnp.bfloat16).astype(jnp.float32)
        low = lse - high - middle
        for k, term in enumerate((high, middle, low)):
            tail = jnp.where(row == k * count + index, jnp.broadcast_to(term, (16, HEAD)), tail)
    return tail.astype(jnp.bfloat16)


def attend_kernel(seqs, table, q_ref, pool_ref, *refs):
    outs = refs[:seqs]
    grouped, gathered, lse_rows, acc = refs[seqs:]
    page_len = pool_ref.shape[2]
    limit = pool_ref.shape[0]
    rows_each = q_ref.shape[1]
    requests = q_ref.shape[0]
    row_count = MEM * rows_each
    at_fill, at_code, at_start, at_slot = limit, 2 * limit, 3 * limit, 3 * limit + 8
    factor = HEAD ** (-0.5) * math.log2(math.e)
    grouped[...] = jnp.zeros_like(grouped)
    for r in range(requests):
        slot = table[at_slot + r]
        grouped[pl.ds(pl.multiple_of(slot * rows_each, rows_each), rows_each), :] = q_ref[r]
    lane_slot = lax.broadcasted_iota(jnp.int32, (1, row_count), 1) // rows_each
    token = lax.broadcasted_iota(jnp.int32, (page_len, row_count), 0)
    for g in range(GROUPS):
        first = table[at_start + g]
        last = table[at_start + g + 1]
        acc[...] = jnp.zeros_like(acc)

        def visit(number, carry):
            old_max, old_sum = carry
            base = first + number * TILE
            places = [jnp.minimum(base + i, limit - 1) for i in range(TILE)]
            keys = jnp.concatenate([pool_ref[table[p], 0] for p in places], 0)
            values = jnp.concatenate([pool_ref[table[p], 1] for p in places], 0)
            scores = lax.dot_general(
                keys,
                grouped[pl.ds(g * row_count, row_count), :],
                (((1,), (1,)), ((), ())),
                preferred_element_type=jnp.float32,
            )
            shown = []
            for i, p in enumerate(places):
                fill = jnp.where(base + i < last, table[at_fill + p], 0)
                code = table[at_code + p]
                rows_ok = jnp.where((lane_slot == code) | (code < 0), fill, 0)
                part = scores[i * page_len : (i + 1) * page_len]
                shown.append(jnp.where(token < rows_ok, part, NEG))
            new_max = old_max
            for part in shown:
                new_max = jnp.maximum(new_max, jnp.max(part, 0, keepdims=True))
            base_max = jnp.where(new_max > 0.5 * NEG, new_max, 0.0)
            fade = jnp.exp2((old_max - base_max) * factor)
            expo = [jnp.exp2((part - base_max) * factor) for part in shown]
            new_sum = old_sum * fade
            for part in expo:
                new_sum = new_sum + jnp.sum(part, 0, keepdims=True)
            weights = jnp.concatenate([part.astype(jnp.bfloat16) for part in expo], 0)
            acc[...] = acc[...] * fade + lax.dot_general(
                values, weights, (((0,), (0,)), ((), ())), preferred_element_type=jnp.float32
            )
            return new_max, new_sum

        start = (
            jnp.full((1, row_count), NEG, jnp.float32),
            jnp.zeros((1, row_count), jnp.float32),
        )
        run_max, run_sum = lax.fori_loop(0, (last - first + TILE - 1) // TILE, visit, start)
        held = run_sum > 0
        safe = jnp.where(held, run_sum, 1.0)
        lse = jnp.where(held, run_max * HEAD ** (-0.5) + jnp.log(safe), NEG)
        gathered[pl.ds(g * row_count, row_count), :] = (acc[...] * (1.0 / safe)).T
        for k in range(row_count // HEAD):
            lse_rows[pl.ds(g * (row_count // HEAD) + k, 1), :] = lse[:, k * HEAD : (k + 1) * HEAD]
    lane = lax.broadcasted_iota(jnp.int32, (8, HEAD), 1) // rows_each
    each = requests // seqs
    per_row = HEAD // rows_each
    for k_out, out_ref in enumerate(outs):
        s = lax.rem(table[at_slot + requests] + k_out, seqs)
        tails = []
        for k in range(each // per_row):
            line = jnp.zeros((8, HEAD), jnp.float32)
            for i in range(per_row):
                r = s * each + k * per_row + i
                slot = table[at_slot + r]
                out_ref[pl.ds((k * per_row + i) * rows_each, rows_each), :] = gathered[
                    pl.ds(pl.multiple_of(slot * rows_each, rows_each), rows_each), :
                ].astype(jnp.bfloat16)
                source = jnp.broadcast_to(lse_rows[pl.ds(slot // per_row, 1), :], (8, HEAD))
                shift = lax.rem(i - lax.rem(slot, per_row) + per_row, per_row) * rows_each
                line = jnp.where(lane == i, pltpu.roll(source, shift, 1), line)
            tails.append(line[0:1])
        out_ref[pl.ds(each * rows_each, 16), :] = packed_tail(tails)


TILE = 8


def attend(table, queries, pool, seqs):
    requests, rows_each, _ = queries.shape
    limit = pool.shape[0] // 2
    own = requests // seqs * rows_each
    return pl.pallas_call(
        functools.partial(attend_kernel, seqs),
        out_shape=[jax.ShapeDtypeStruct((own + 16, HEAD), jnp.bfloat16)] * seqs,
        grid_spec=pltpu.PrefetchScalarGridSpec(
            num_scalar_prefetch=1,
            grid=(1,),
            in_specs=[
                pl.BlockSpec((requests, rows_each, HEAD), lambda i, t: (0, 0, 0)),
                pl.BlockSpec((limit,) + pool.shape[1:], lambda i, t: (0, 0, 0, 0)),
            ],
            out_specs=[pl.BlockSpec((own + 16, HEAD), lambda i, t: (0, 0))] * seqs,
            scratch_shapes=[
                pltpu.VMEM((GROUPS * MEM * rows_each, HEAD), jnp.bfloat16),
                pltpu.VMEM((GROUPS * MEM * rows_each, HEAD), jnp.float32),
                pltpu.VMEM((GROUPS * MEM * rows_each // HEAD, HEAD), jnp.float32),
                pltpu.VMEM((HEAD, MEM * rows_each), jnp.float32),
            ],
        ),
        cost_estimate=pl.CostEstimate(
            flops=4 * limit * 64 * MEM * rows_each * HEAD,
            bytes_accessed=limit * 2 * 64 * HEAD * 2,
            transcendentals=limit * 64 * MEM * rows_each,
        ),
        name="attend",
    )(table, queries, pool)


def fresh_kernel(steps, q_ref, k_ref, v_ref, out_ref):
    rows = q_ref.shape[0]
    count = k_ref.shape[0] // steps
    rows_each = rows // count
    shape = (steps * count, rows)
    key = lax.broadcasted_iota(jnp.int32, shape, 0)
    lane = lax.broadcasted_iota(jnp.int32, shape, 1)
    seen = (lane // rows_each == lax.rem(key, count)) & (
        key // count <= lax.rem(lane, rows_each) // (rows_each // steps)
    )
    scores = lax.dot_general(
        k_ref[...], q_ref[...], (((1,), (1,)), ((), ())), preferred_element_type=jnp.float32
    ) * HEAD ** (-0.5)
    scores = jnp.where(seen, scores, NEG)
    peak = jnp.max(scores, 0, keepdims=True)
    expo = jnp.where(seen, jnp.exp(scores - peak), 0.0)
    total = jnp.sum(expo, 0, keepdims=True)
    value = lax.dot_general(
        v_ref[...],
        expo.astype(jnp.bfloat16),
        (((0,), (0,)), ((), ())),
        preferred_element_type=jnp.float32,
    )
    out_ref[pl.ds(0, rows), :] = (value * (1.0 / total)).T.astype(jnp.bfloat16)
    lse = peak + jnp.log(total)
    out_ref[pl.ds(rows, 16), :] = packed_tail(
        [lse[:, k * HEAD : (k + 1) * HEAD] for k in range(rows // HEAD)]
    )


def fresh_part(queries, keys, values, steps):
    rows = queries.shape[0]
    return pl.pallas_call(
        functools.partial(fresh_kernel, steps),
        out_shape=jax.ShapeDtypeStruct((rows + 16, HEAD), jnp.bfloat16),
        cost_estimate=pl.CostEstimate(
            flops=4 * rows * keys.shape[0] * HEAD, bytes_accessed=rows * HEAD * 4, transcendentals=0
        ),
        name="fresh",
    )(queries, keys, values)


def mix_refs(parts):
    rows = parts[0].shape[0] - 16
    blocks = rows // HEAD
    lses = []
    for part in parts:
        tail = part[pl.ds(rows, 16), :].astype(jnp.float32)
        lses.append(
            tail[0:blocks] + tail[blocks : 2 * blocks] + tail[2 * blocks : 3 * blocks]
        )
    peak = lses[0]
    for lse in lses[1:]:
        peak = jnp.maximum(peak, lse)
    fades = [jnp.exp(lse - peak) for lse in lses]
    total = sum(fades)
    inverse = 1.0 / total
    turned = [
        jnp.concatenate([fade * inverse, jnp.zeros((8 - blocks, HEAD), jnp.float32)], 0).T
        for fade in fades
    ]
    values = []
    for k in range(blocks):
        value = 0.0
        for part, weight in zip(parts, turned):
            value = value + part[pl.ds(k * HEAD, HEAD), :].astype(jnp.float32) * weight[:, k : k + 1]
        values.append(value)
    return values, peak + jnp.log(total)


def mix_kernel(*refs):
    out_ref = refs[-1]
    values, lse = mix_refs(refs[:-1])
    for k, value in enumerate(values):
        out_ref[pl.ds(k * HEAD, HEAD), :] = value.astype(jnp.bfloat16)
    out_ref[pl.ds(len(values) * HEAD, 16), :] = packed_tail(
        [lse[k : k + 1] for k in range(len(values))]
    )


def mix(parts):
    return pl.pallas_call(
        mix_kernel,
        out_shape=jax.ShapeDtypeStruct(parts[0].shape, jnp.bfloat16),
        cost_estimate=pl.CostEstimate(
            flops=2 * len(parts) * parts[0].size, bytes_accessed=parts[0].size * 10, transcendentals=0
        ),
        name="mix",
    )(*parts)


def final_kernel(ratio, *refs):
    parts, out_ref, scratch = refs[:-2], refs[-2], refs[-1]
    values, _ = mix_refs(parts)
    for k, value in enumerate(values):
        scratch[pl.ds(k * HEAD, HEAD), :] = value
    tokens = out_ref.shape[0]
    for h in range(ratio):
        out_ref[:, h * HEAD : (h + 1) * HEAD] = scratch[pl.ds(h, tokens, stride=ratio), :].astype(
            jnp.bfloat16
        )


def final(parts, ratio):
    rows = parts[0].shape[0] - 16
    return pl.pallas_call(
        functools.partial(final_kernel, ratio),
        out_shape=jax.ShapeDtypeStruct((rows // ratio, ratio * HEAD), jnp.bfloat16),
        scratch_shapes=[pltpu.VMEM((rows, HEAD), jnp.float32)],
        cost_estimate=pl.CostEstimate(
            flops=2 * len(parts) * parts[0].size, bytes_accessed=parts[0].size * 10, transcendentals=0
        ),
        name="final",
    )(*parts)


def page_table(owners, fills, group_of_request):
    requests = group_of_request.shape[0]
    count = owners.shape[0]
    index = jnp.arange(requests, dtype=jnp.int32)
    same = group_of_request[:, None] == group_of_request[None, :]
    rank = jnp.sum((same & (index[None, :] < index[:, None])).astype(jnp.int32), 1)
    slot = group_of_request * MEM + rank
    shared = owners >= requests
    own_slot = jnp.sum(jnp.where(owners[:, None] == index[None, :], slot[None, :], 0), 1)
    group = jnp.where(shared, owners - requests, own_slot // MEM)
    group = jnp.where(owners >= 0, group, GROUPS)
    code = jnp.where(shared, -1, own_slot % MEM)
    place = jnp.arange(count, dtype=jnp.int32)
    before = (group[None, :] < group[:, None]) | (
        (group[None, :] == group[:, None]) & (place[None, :] < place[:, None])
    )
    target = jnp.sum(before.astype(jnp.int32), 1)
    hit = target[None, :] == place[:, None]
    ordered = [
        jnp.sum(jnp.where(hit, row[None, :], 0), 1) for row in (place, fills, code)
    ]
    starts = jnp.sum(
        (group[None, :] < jnp.arange(8, dtype=jnp.int32)[:, None]).astype(jnp.int32), 1
    )
    return jnp.concatenate(ordered + [starts, slot, lax.axis_index("seq").astype(jnp.int32)[None]])


CAP_SEQ = 44
CAP_ROW = 40


def earlier(count):
    index = jnp.arange(count, dtype=jnp.int32)
    return index[None, :] < index[:, None]


def counted(mask, axis):
    return jnp.sum(mask.astype(jnp.int32), axis)


def inverted(place, value, count):
    hit = place[None, :] == jnp.arange(count, dtype=jnp.int32)[:, None]
    return jnp.sum(jnp.where(hit, value[None, :], 0), 1)


def migration_tables(page_owner, migrate_dest, pool_size):
    rows, seqs = lax.axis_size("row"), lax.axis_size("seq")
    row, seq = lax.axis_index("row"), lax.axis_index("seq")
    limit = pool_size // 2
    cap = pool_size // (rows * seqs)
    dest = migrate_dest.reshape(rows, seqs, pool_size)[:, :, :limit]
    live = (page_owner >= 0).reshape(rows, seqs, pool_size)[:, :, :limit]
    dest = jnp.where(live, dest, -1)
    column = jnp.where(live, dest % seqs, -1)
    all_seq = jnp.arange(seqs, dtype=jnp.int32)
    in_column = counted(column[..., None, :] == all_seq[:, None], -1)
    everyone = jnp.arange(rows * seqs, dtype=jnp.int32)
    from_row = counted(dest.reshape(rows, 1, seqs * limit) == everyone[:, None], -1)
    fits = (jnp.max(in_column) <= CAP_SEQ) & (jnp.max(from_row) <= CAP_ROW)

    dest_row = lax.dynamic_index_in_dim(dest, row, 0, False)
    own = lax.dynamic_index_in_dim(dest_row, seq, 0, False)
    step = jnp.where(own >= 0, (own % seqs - seq + seqs) % seqs, -1)
    rank = counted((step[None, :] == step[:, None]) & earlier(limit), 1)
    place = jnp.where((step >= 0) & (rank < CAP_SEQ), step * CAP_SEQ + rank, -1)
    first = inverted(place, jnp.arange(limit, dtype=jnp.int32), seqs * CAP_SEQ)

    sender = (seq - all_seq + seqs) % seqs
    lists = jnp.sum(
        jnp.where((sender[:, None] == all_seq[None, :])[..., None], dest_row[None], 0), 1
    )
    lists = lists.reshape(seqs * limit)
    which = jnp.arange(seqs * limit, dtype=jnp.int32) // limit
    here = (lists >= 0) & (lists % seqs == seq)
    step = jnp.where(here, (lists // seqs - row + rows) % rows, -1)
    before = earlier(seqs * limit) & here[None, :]
    rank = counted(before & (which[None, :] == which[:, None]), 1)
    order = counted(before & (step[None, :] == step[:, None]), 1)
    place = jnp.where(here & (order < CAP_ROW), step * CAP_ROW + order, -1)
    second = inverted(place, which * CAP_SEQ + jnp.minimum(rank, CAP_SEQ - 1), rows * CAP_ROW)

    coming = counted(dest == row * seqs + seq, -1)
    ahead = (seq - all_seq + seqs) % seqs
    offset = jnp.sum(jnp.where(ahead[None, :] < ahead[:, None], coming[:, None, :], 0), -1)
    listed = (row - jnp.arange(rows, dtype=jnp.int32) + rows) % rows
    page = jnp.arange(cap, dtype=jnp.int32)
    third = (listed[:, None] * CAP_ROW + offset)[..., None] + page
    third = jnp.where(page < coming[..., None], jnp.minimum(third, rows * CAP_ROW - 1), -1)
    return fits, first, second, third.reshape(pool_size), coming.reshape(rows * seqs)


def split_kernel(table, pool_ref, *refs):
    out_refs, scratch, arrived, sems = refs[:-3], refs[-3], refs[-2], refs[-1]
    lists = len(out_refs) // 2
    length = out_refs[0].shape[0]
    copy = pltpu.make_async_copy(pool_ref.at[pl.ds(0, scratch.shape[0])], scratch, arrived)
    copy.start()
    copy.wait()
    for k in range(lists):

        def move(i, _):
            page = table[k * length + i]
            for half in range(2):
                pltpu.make_async_copy(
                    scratch.at[page, half], out_refs[half * lists + k].at[i], sems.at[half * lists + k]
                ).start()
            return 0

        lax.fori_loop(0, length, move, 0, unroll=4)
    for k, out in enumerate(out_refs):
        pltpu.make_async_copy(out, out, sems.at[k]).wait()


def split_pool(table, pool, lists):
    limit, _, page_len, width = (pool.shape[0] // 2,) + pool.shape[1:]
    length = table.shape[0] // lists
    shape = (length, page_len, width)
    return pl.pallas_call(
        split_kernel,
        out_shape=[jax.ShapeDtypeStruct(shape, pool.dtype)] * (2 * lists),
        grid_spec=pltpu.PrefetchScalarGridSpec(
            num_scalar_prefetch=1,
            grid=(1,),
            in_specs=[pl.BlockSpec(memory_space=pl.ANY)],
            out_specs=[pl.BlockSpec(memory_space=pl.ANY)] * (2 * lists),
            scratch_shapes=[
                pltpu.VMEM((limit,) + pool.shape[1:], pool.dtype),
                pltpu.SemaphoreType.DMA,
                pltpu.SemaphoreType.DMA((2 * lists,)),
            ],
        ),
        cost_estimate=pl.CostEstimate(
            flops=0, bytes_accessed=pool.size + 4 * lists * length * page_len * width, transcendentals=0
        ),
        name="split_pool",
    )(table, pool)


def resplit_kernel(count, table, *refs):
    sources, outs = refs[:count], refs[count : 2 * count]
    scratch, arrived, sems = refs[2 * count :]
    length = sources[0].shape[0]
    copies = [
        pltpu.make_async_copy(ref, scratch.at[pl.ds(k * length, length)], arrived.at[k])
        for k, ref in enumerate(sources)
    ]
    for copy in copies:
        copy.start()
    for copy in copies:
        copy.wait()
    length_out = outs[0].shape[0]
    for k, out in enumerate(outs):

        def move(i, _):
            pltpu.make_async_copy(
                scratch.at[table[k * length_out + i]], out.at[i], sems.at[k]
            ).start()
            return 0

        lax.fori_loop(0, length_out, move, 0, unroll=4)
    for k, out in enumerate(outs):
        pltpu.make_async_copy(out, out, sems.at[k]).wait()


def resplit(table, lists):
    count = len(lists)
    length, page_len, width = lists[0].shape
    shape = (table.shape[0] // count, page_len, width)
    return pl.pallas_call(
        functools.partial(resplit_kernel, count),
        out_shape=[jax.ShapeDtypeStruct(shape, lists[0].dtype)] * count,
        grid_spec=pltpu.PrefetchScalarGridSpec(
            num_scalar_prefetch=1,
            grid=(1,),
            in_specs=[pl.BlockSpec(memory_space=pl.ANY)] * count,
            out_specs=[pl.BlockSpec(memory_space=pl.ANY)] * count,
            scratch_shapes=[
                pltpu.VMEM((count * length, page_len, width), lists[0].dtype),
                pltpu.SemaphoreType.DMA((count,)),
                pltpu.SemaphoreType.DMA((count,)),
            ],
        ),
        cost_estimate=pl.CostEstimate(
            flops=0, bytes_accessed=4 * count * length * page_len * width, transcendentals=0
        ),
        name="resplit",
    )(table, *lists)


def settle_kernel(count, table, *refs):
    sources, out, scratch, zero, sems, done = refs[: 2 * count], refs[-5], refs[-4], refs[-3], refs[-2], refs[-1]
    length = sources[0].shape[0]
    copies = [
        pltpu.make_async_copy(
            ref, scratch.at[k // count, pl.ds(k % count * length, length)], sems.at[k]
        )
        for k, ref in enumerate(sources)
    ]
    for copy in copies:
        copy.start()
    zero[...] = jnp.zeros_like(zero)
    for copy in copies:
        copy.wait()

    def place_page(i, _):
        place = table[i]

        @pl.when(place >= 0)
        def _():
            for half in range(2):
                pltpu.make_async_copy(scratch.at[half, place], out.at[i, half], done).start()

        @pl.when(place < 0)
        def _():
            pltpu.make_async_copy(zero, out.at[i], done).start()

        return 0

    lax.fori_loop(0, out.shape[0], place_page, 0, unroll=4)
    pltpu.make_async_copy(out, out, done).wait()


def settle(table, keys, values):
    count = len(keys)
    length, page_len, width = keys[0].shape
    slots = table.shape[0]
    kind = keys[0].dtype
    return pl.pallas_call(
        functools.partial(settle_kernel, count),
        out_shape=jax.ShapeDtypeStruct((slots, 2, page_len, width), kind),
        grid_spec=pltpu.PrefetchScalarGridSpec(
            num_scalar_prefetch=1,
            grid=(1,),
            in_specs=[pl.BlockSpec(memory_space=pl.ANY)] * (2 * count),
            out_specs=pl.BlockSpec(memory_space=pl.ANY),
            scratch_shapes=[
                pltpu.VMEM((2, count * length, page_len, width), kind),
                pltpu.VMEM((2, page_len, width), kind),
                pltpu.SemaphoreType.DMA((2 * count,)),
                pltpu.SemaphoreType.DMA,
            ],
        ),
        cost_estimate=pl.CostEstimate(
            flops=0, bytes_accessed=8 * slots * page_len * width, transcendentals=0
        ),
        name="settle",
    )(table, *keys, *values)


def passed(lists, axis):
    return [lists[0]] + [
        lax.ppermute(part, axis, ring(axis, k)) for k, part in enumerate(lists) if k
    ]


def rotate(values, cosine, sine):
    half = values.shape[-1] // 2
    first_half = values[..., :half]
    second_half = values[..., half:]
    return jnp.concatenate(
        [first_half * cosine - second_half * sine, second_half * cosine + first_half * sine], -1
    )


def migrate_whole(kv_pool, migrate_dest, coming, device):
    pool_size = kv_pool.shape[0]
    own_dest = lax.dynamic_slice_in_dim(migrate_dest, device * pool_size, pool_size)
    send_order = jnp.argsort(own_dest, stable=True)
    moved = lax.all_to_all(
        kv_pool[send_order], ("row", "seq"), split_axis=0, concat_axis=0, tiled=True
    )
    page = jnp.arange(pool_size // coming.shape[0], dtype=jnp.int32)
    full = (page[None, :] < coming[:, None]).reshape(pool_size)
    return jnp.where(full[:, None, None, None], moved, jnp.zeros_like(moved))


def block(
    hidden_in,
    norm_gain,
    w_qkv,
    w_out,
    kv_pool,
    page_owner,
    page_fill,
    lengths,
    group_of_request,
    migrate_dest,
):
    step_count, request_count, width_here = hidden_in.shape
    ratio = HEADS // KV_HEADS
    heads_here = w_qkv.shape[1] // ((ratio + 2) * HEAD)
    fits, first_table, second_table, third_table, coming = migration_tables(
        page_owner, migrate_dest, kv_pool.shape[0]
    )
    first_table, hidden_in = lax.optimization_barrier((first_table, hidden_in))
    hidden_f = hidden_in.astype(jnp.float32)
    seqs = lax.axis_size("seq")
    lists = split_pool(first_table, kv_pool, seqs)
    key_lists = passed(lists[:seqs], "seq")
    value_lists = passed(lists[seqs:], "seq")
    row_start = lax.axis_index("row") * width_here
    gain_f = lax.dynamic_slice_in_dim(norm_gain, row_start, width_here).astype(jnp.float32)
    width = width_here * lax.axis_size("row")
    squares = jnp.sum(hidden_f * hidden_f, -1)
    partial_value = jnp.dot(
        (hidden_f * gain_f).astype(jnp.bfloat16).reshape(step_count * request_count, width_here),
        w_qkv,
        preferred_element_type=jnp.float32,
    ).astype(jnp.bfloat16)
    partial_value, page_fill, group_of_request = lax.optimization_barrier(
        (partial_value, page_fill, group_of_request)
    )
    columns = partial_value.shape[1]
    extra = jnp.pad(jnp.stack(pieces(squares), -1), ((0, 0), (0, 0), (0, HEAD - 3)))
    partial_value = jnp.concatenate(
        [partial_value.reshape(step_count, request_count, columns), extra], 2
    )
    step_here = lax.axis_index("row")
    position = (lengths + step_here).astype(jnp.float32)
    half = HEAD // 2
    angle = position[:, None] * THETA ** (-(jnp.arange(half, dtype=jnp.float32) * 2.0 / HEAD))
    cosine, sine = lax.optimization_barrier((jnp.cos(angle), jnp.sin(angle)))
    summed = lax.dynamic_index_in_dim(partial_value, step_here, 0, False).astype(jnp.float32)
    arrived = exchanged(partial_value, "row")
    for part in arrived:
        summed = summed + part.astype(jnp.float32)
    scale = lax.rsqrt(jnp.sum(summed[:, columns : columns + 3], -1) / width + EPS)
    projected = (summed[:, :columns] * scale[:, None]).astype(jnp.bfloat16).astype(jnp.float32)
    projected = projected.reshape(request_count, heads_here * (ratio + 2), HEAD)
    rotated = rotate(projected, cosine[:, None], sine[:, None])
    is_value = jnp.arange(heads_here * (ratio + 2)) % (ratio + 2) == ratio + 1
    ready = jnp.where(is_value[None, :, None], projected, rotated).astype(jnp.bfloat16)
    ready = collected(ready, "row")
    ready = ready.reshape(step_count, request_count, heads_here, ratio + 2, HEAD)
    key_lists = resplit(second_table, key_lists)
    key_lists = passed(key_lists, "row")
    queries = ready[:, :, :, :ratio]
    keys_new = ready[:, :, :, ratio]
    values_new = ready[:, :, :, ratio + 1]
    local_req = request_count // lax.axis_size("seq")
    req_start = lax.axis_index("seq") * local_req
    new_kv = jnp.stack(
        [
            keys_new.reshape(step_count, request_count, heads_here * HEAD),
            values_new.reshape(step_count, request_count, heads_here * HEAD),
        ],
        2,
    )
    new_kv_local = lax.dynamic_slice_in_dim(new_kv, req_start, local_req, 1)
    device = lax.axis_index("row") * lax.axis_size("seq") + lax.axis_index("seq")
    pool_size = kv_pool.shape[0]
    owners_here = lax.dynamic_slice_in_dim(page_owner, device * pool_size, pool_size)
    fills = lax.dynamic_slice_in_dim(page_fill, device * pool_size, pool_size)
    live_limit = pool_size // 2
    table = page_table(owners_here[:live_limit], fills[:live_limit], group_of_request)
    rows_here = step_count * ratio
    rows_first = queries[:, :, 0].transpose(1, 0, 2, 3).reshape(request_count, rows_here, HEAD)
    seq_size = lax.axis_size("seq")
    own_rows = local_req * rows_here
    both = attend(table, rows_first, kv_pool, seq_size)
    parts = passed(both, "seq")
    query_own = lax.dynamic_slice_in_dim(rows_first, req_start, local_req, 0)
    key_own = lax.dynamic_slice_in_dim(keys_new, req_start, local_req, 1)
    value_own = lax.dynamic_slice_in_dim(values_new, req_start, local_req, 1)
    own = fresh_part(
        query_own.reshape(own_rows, HEAD),
        key_own.reshape(step_count * local_req, HEAD),
        value_own.reshape(step_count * local_req, HEAD),
        step_count,
    )
    value_lists = resplit(second_table, value_lists)
    both = mix(parts)
    parts = [both] + [lax.ppermute(both, "row", ring("row", k)) for k in range(1, 4)]
    value_lists = passed(value_lists, "row")
    picked = final([own] + parts, ratio)
    partial_out = jnp.dot(picked, w_out, preferred_element_type=jnp.float32).astype(jnp.bfloat16)
    col_size = lax.axis_size("col")
    col_width = partial_out.shape[1] // col_size
    spread = partial_out.reshape(step_count * local_req, col_size, col_width).transpose(1, 0, 2)
    summed = jnp.sum(
        lax.all_to_all(spread, "col", 0, 0, tiled=True).astype(jnp.float32), 0
    )
    residual = lax.dynamic_slice_in_dim(
        lax.dynamic_slice_in_dim(hidden_f, req_start, local_req, 1),
        lax.axis_index("col") * col_width,
        col_width,
        2,
    )
    summed = summed.reshape(local_req, step_count, col_width).transpose(1, 0, 2)
    layer_out = (summed + residual).astype(jnp.bfloat16)
    moved = lax.cond(
        fits,
        lambda: settle(third_table, key_lists, value_lists),
        lambda: migrate_whole(kv_pool, migrate_dest, coming, device),
    )
    return (layer_out, new_kv_local, moved)


def solution(mesh):
    in_specs = (
        P(None, None, "row"),
        P(),
        P("row", "col"),
        P("col", "row"),
        P(("row", "seq"), None, None, "col"),
        P(),
        P(),
        P(),
        P(),
        P(),
    )
    out_specs = (
        P(None, "seq", ("row", "col")),
        P(None, "seq", None, "col"),
        P(("row", "seq"), None, None, "col"),
    )
    return jax.shard_map(block, mesh=mesh, in_specs=in_specs, out_specs=out_specs, check_vma=False)
```

```python
import functools
import math

import jax
import jax.numpy as jnp
from jax import lax
from jax.experimental import pallas as pl
from jax.experimental.pallas import tpu as pltpu
from jax.sharding import PartitionSpec as P

HEADS = 64
KV_HEADS = 8
HEAD = 128
GROUPS = 4
MEM = 16


EPS = 1e-06
THETA = 1000000.0
NEG = -1e30


def ring(axis, step):
    size = lax.axis_size(axis)
    return [(k, (k + step) % size) for k in range(size)]


def exchanged(parts, axis):
    size = lax.axis_size(axis)
    here = lax.axis_index(axis)
    return [
        lax.ppermute(
            lax.dynamic_index_in_dim(parts, (here + step) % size, 0, False), axis, ring(axis, step)
        )
        for step in range(1, size)
    ]


def collected(part, axis):
    size = lax.axis_size(axis)
    here = lax.axis_index(axis)
    ahead = [part] + [lax.ppermute(part, axis, ring(axis, size - step)) for step in range(1, size)]
    twice = jnp.stack(ahead + ahead[:-1])
    return lax.dynamic_slice_in_dim(twice, (size - here) % size, size, 0)


def pieces(value):
    high = lax.reduce_precision(value, 8, 7)
    middle = lax.reduce_precision(value - high, 8, 7)
    low = value - high - middle
    return [high.astype(jnp.bfloat16), middle.astype(jnp.bfloat16), low.astype(jnp.bfloat16)]


def packed_tail(lse_rows):
    count = len(lse_rows)
    row = lax.broadcasted_iota(jnp.int32, (16, HEAD), 0)
    tail = jnp.zeros((16, HEAD), jnp.float32)
    for index, lse in enumerate(lse_rows):
        high = lse.astype(jnp.bfloat16).astype(jnp.float32)
        middle = (lse - high).astype(jnp.bfloat16).astype(jnp.float32)
        low = lse - high - middle
        for k, term in enumerate((high, middle, low)):
            tail = jnp.where(row == k * count + index, jnp.broadcast_to(term, (16, HEAD)), tail)
    return tail.astype(jnp.bfloat16)


def attend_kernel(seqs, table, q_ref, pool_ref, *refs):
    outs = refs[:seqs]
    grouped, gathered, lse_rows, acc = refs[seqs:]
    page_len = pool_ref.shape[2]
    limit = pool_ref.shape[0]
    rows_each = q_ref.shape[1]
    requests = q_ref.shape[0]
    row_count = MEM * rows_each
    at_fill, at_code, at_start, at_slot = limit, 2 * limit, 3 * limit, 3 * limit + 8
    factor = HEAD ** (-0.5) * math.log2(math.e)
    grouped[...] = jnp.zeros_like(grouped)
    for r in range(requests):
        slot = table[at_slot + r]
        grouped[pl.ds(pl.multiple_of(slot * rows_each, rows_each), rows_each), :] = q_ref[r]
    lane_slot = lax.broadcasted_iota(jnp.int32, (1, row_count), 1) // rows_each
    token = lax.broadcasted_iota(jnp.int32, (page_len, row_count), 0)
    for g in range(GROUPS):
        first = table[at_start + g]
        last = table[at_start + g + 1]
        acc[...] = jnp.zeros_like(acc)

        def visit(number, carry):
            old_max, old_sum = carry
            base = first + number * TILE
            places = [jnp.minimum(base + i, limit - 1) for i in range(TILE)]
            keys = jnp.concatenate([pool_ref[table[p], 0] for p in places], 0)
            values = jnp.concatenate([pool_ref[table[p], 1] for p in places], 0)
            scores = lax.dot_general(
                keys,
                grouped[pl.ds(g * row_count, row_count), :],
                (((1,), (1,)), ((), ())),
                preferred_element_type=jnp.float32,
            )
            shown = []
            for i, p in enumerate(places):
                fill = jnp.where(base + i < last, table[at_fill + p], 0)
                code = table[at_code + p]
                rows_ok = jnp.where((lane_slot == code) | (code < 0), fill, 0)
                part = scores[i * page_len : (i + 1) * page_len]
                shown.append(jnp.where(token < rows_ok, part, NEG))
            new_max = old_max
            for part in shown:
                new_max = jnp.maximum(new_max, jnp.max(part, 0, keepdims=True))
            base_max = jnp.where(new_max > 0.5 * NEG, new_max, 0.0)
            fade = jnp.exp2((old_max - base_max) * factor)
            expo = [jnp.exp2((part - base_max) * factor) for part in shown]
            new_sum = old_sum * fade
            for part in expo:
                new_sum = new_sum + jnp.sum(part, 0, keepdims=True)
            weights = jnp.concatenate([part.astype(jnp.bfloat16) for part in expo], 0)
            acc[...] = acc[...] * fade + lax.dot_general(
                values, weights, (((0,), (0,)), ((), ())), preferred_element_type=jnp.float32
            )
            return new_max, new_sum

        start = (
            jnp.full((1, row_count), NEG, jnp.float32),
            jnp.zeros((1, row_count), jnp.float32),
        )
        run_max, run_sum = lax.fori_loop(0, (last - first + TILE - 1) // TILE, visit, start)
        held = run_sum > 0
        safe = jnp.where(held, run_sum, 1.0)
        lse = jnp.where(held, run_max * HEAD ** (-0.5) + jnp.log(safe), NEG)
        gathered[pl.ds(g * row_count, row_count), :] = (acc[...] * (1.0 / safe)).T
        for k in range(row_count // HEAD):
            lse_rows[pl.ds(g * (row_count // HEAD) + k, 1), :] = lse[:, k * HEAD : (k + 1) * HEAD]
    lane = lax.broadcasted_iota(jnp.int32, (8, HEAD), 1) // rows_each
    each = requests // seqs
    per_row = HEAD // rows_each
    for k_out, out_ref in enumerate(outs):
        s = lax.rem(table[at_slot + requests] + k_out, seqs)
        tails = []
        for k in range(each // per_row):
            line = jnp.zeros((8, HEAD), jnp.float32)
            for i in range(per_row):
                r = s * each + k * per_row + i
                slot = table[at_slot + r]
                out_ref[pl.ds((k * per_row + i) * rows_each, rows_each), :] = gathered[
                    pl.ds(pl.multiple_of(slot * rows_each, rows_each), rows_each), :
                ].astype(jnp.bfloat16)
                source = jnp.broadcast_to(lse_rows[pl.ds(slot // per_row, 1), :], (8, HEAD))
                shift = lax.rem(i - lax.rem(slot, per_row) + per_row, per_row) * rows_each
                line = jnp.where(lane == i, pltpu.roll(source, shift, 1), line)
            tails.append(line[0:1])
        out_ref[pl.ds(each * rows_each, 16), :] = packed_tail(tails)


TILE = 8


def attend(table, queries, pool, seqs):
    requests, rows_each, _ = queries.shape
    limit = pool.shape[0] // 2
    own = requests // seqs * rows_each
    return pl.pallas_call(
        functools.partial(attend_kernel, seqs),
        out_shape=[jax.ShapeDtypeStruct((own + 16, HEAD), jnp.bfloat16)] * seqs,
        grid_spec=pltpu.PrefetchScalarGridSpec(
            num_scalar_prefetch=1,
            grid=(1,),
            in_specs=[
                pl.BlockSpec((requests, rows_each, HEAD), lambda i, t: (0, 0, 0)),
                pl.BlockSpec((limit,) + pool.shape[1:], lambda i, t: (0, 0, 0, 0)),
            ],
            out_specs=[pl.BlockSpec((own + 16, HEAD), lambda i, t: (0, 0))] * seqs,
            scratch_shapes=[
                pltpu.VMEM((GROUPS * MEM * rows_each, HEAD), jnp.bfloat16),
                pltpu.VMEM((GROUPS * MEM * rows_each, HEAD), jnp.float32),
                pltpu.VMEM((GROUPS * MEM * rows_each // HEAD, HEAD), jnp.float32),
                pltpu.VMEM((HEAD, MEM * rows_each), jnp.float32),
            ],
        ),
        cost_estimate=pl.CostEstimate(
            flops=4 * limit * 64 * MEM * rows_each * HEAD,
            bytes_accessed=limit * 2 * 64 * HEAD * 2,
            transcendentals=limit * 64 * MEM * rows_each,
        ),
        name="attend",
    )(table, queries, pool)


def fresh_kernel(steps, q_ref, k_ref, v_ref, out_ref):
    rows = q_ref.shape[0]
    count = k_ref.shape[0] // steps
    rows_each = rows // count
    shape = (steps * count, rows)
    key = lax.broadcasted_iota(jnp.int32, shape, 0)
    lane = lax.broadcasted_iota(jnp.int32, shape, 1)
    seen = (lane // rows_each == lax.rem(key, count)) & (
        key // count <= lax.rem(lane, rows_each) // (rows_each // steps)
    )
    scores = lax.dot_general(
        k_ref[...], q_ref[...], (((1,), (1,)), ((), ())), preferred_element_type=jnp.float32
    ) * HEAD ** (-0.5)
    scores = jnp.where(seen, scores, NEG)
    peak = jnp.max(scores, 0, keepdims=True)
    expo = jnp.where(seen, jnp.exp(scores - peak), 0.0)
    total = jnp.sum(expo, 0, keepdims=True)
    value = lax.dot_general(
        v_ref[...],
        expo.astype(jnp.bfloat16),
        (((0,), (0,)), ((), ())),
        preferred_element_type=jnp.float32,
    )
    out_ref[pl.ds(0, rows), :] = (value * (1.0 / total)).T.astype(jnp.bfloat16)
    lse = peak + jnp.log(total)
    out_ref[pl.ds(rows, 16), :] = packed_tail(
        [lse[:, k * HEAD : (k + 1) * HEAD] for k in range(rows // HEAD)]
    )


def fresh_part(queries, keys, values, steps):
    rows = queries.shape[0]
    return pl.pallas_call(
        functools.partial(fresh_kernel, steps),
        out_shape=jax.ShapeDtypeStruct((rows + 16, HEAD), jnp.bfloat16),
        cost_estimate=pl.CostEstimate(
            flops=4 * rows * keys.shape[0] * HEAD, bytes_accessed=rows * HEAD * 4, transcendentals=0
        ),
        name="fresh",
    )(queries, keys, values)


def mix_refs(parts):
    rows = parts[0].shape[0] - 16
    blocks = rows // HEAD
    lses = []
    for part in parts:
        tail = part[pl.ds(rows, 16), :].astype(jnp.float32)
        lses.append(
            tail[0:blocks] + tail[blocks : 2 * blocks] + tail[2 * blocks : 3 * blocks]
        )
    peak = lses[0]
    for lse in lses[1:]:
        peak = jnp.maximum(peak, lse)
    fades = [jnp.exp(lse - peak) for lse in lses]
    total = sum(fades)
    inverse = 1.0 / total
    turned = [
        jnp.concatenate([fade * inverse, jnp.zeros((8 - blocks, HEAD), jnp.float32)], 0).T
        for fade in fades
    ]
    values = []
    for k in range(blocks):
        value = 0.0
        for part, weight in zip(parts, turned):
            value = value + part[pl.ds(k * HEAD, HEAD), :].astype(jnp.float32) * weight[:, k : k + 1]
        values.append(value)
    return values, peak + jnp.log(total)


def mix_kernel(*refs):
    out_ref = refs[-1]
    values, lse = mix_refs(refs[:-1])
    for k, value in enumerate(values):
        out_ref[pl.ds(k * HEAD, HEAD), :] = value.astype(jnp.bfloat16)
    out_ref[pl.ds(len(values) * HEAD, 16), :] = packed_tail(
        [lse[k : k + 1] for k in range(len(values))]
    )


def mix(parts):
    return pl.pallas_call(
        mix_kernel,
        out_shape=jax.ShapeDtypeStruct(parts[0].shape, jnp.bfloat16),
        cost_estimate=pl.CostEstimate(
            flops=2 * len(parts) * parts[0].size, bytes_accessed=parts[0].size * 10, transcendentals=0
        ),
        name="mix",
    )(*parts)


def final_kernel(ratio, *refs):
    parts, out_ref, scratch = refs[:-2], refs[-2], refs[-1]
    values, _ = mix_refs(parts)
    for k, value in enumerate(values):
        scratch[pl.ds(k * HEAD, HEAD), :] = value
    tokens = out_ref.shape[0]
    for h in range(ratio):
        out_ref[:, h * HEAD : (h + 1) * HEAD] = scratch[pl.ds(h, tokens, stride=ratio), :].astype(
            jnp.bfloat16
        )


def final(parts, ratio):
    rows = parts[0].shape[0] - 16
    return pl.pallas_call(
        functools.partial(final_kernel, ratio),
        out_shape=jax.ShapeDtypeStruct((rows // ratio, ratio * HEAD), jnp.bfloat16),
        scratch_shapes=[pltpu.VMEM((rows, HEAD), jnp.float32)],
        cost_estimate=pl.CostEstimate(
            flops=2 * len(parts) * parts[0].size, bytes_accessed=parts[0].size * 10, transcendentals=0
        ),
        name="final",
    )(*parts)


def page_table(owners, fills, group_of_request):
    requests = group_of_request.shape[0]
    count = owners.shape[0]
    index = jnp.arange(requests, dtype=jnp.int32)
    same = group_of_request[:, None] == group_of_request[None, :]
    rank = jnp.sum((same & (index[None, :] < index[:, None])).astype(jnp.int32), 1)
    slot = group_of_request * MEM + rank
    shared = owners >= requests
    own_slot = jnp.sum(jnp.where(owners[:, None] == index[None, :], slot[None, :], 0), 1)
    group = jnp.where(shared, owners - requests, own_slot // MEM)
    group = jnp.where(owners >= 0, group, GROUPS)
    code = jnp.where(shared, -1, own_slot % MEM)
    place = jnp.arange(count, dtype=jnp.int32)
    before = (group[None, :] < group[:, None]) | (
        (group[None, :] == group[:, None]) & (place[None, :] < place[:, None])
    )
    target = jnp.sum(before.astype(jnp.int32), 1)
    hit = target[None, :] == place[:, None]
    ordered = [
        jnp.sum(jnp.where(hit, row[None, :], 0), 1) for row in (place, fills, code)
    ]
    starts = jnp.sum(
        (group[None, :] < jnp.arange(8, dtype=jnp.int32)[:, None]).astype(jnp.int32), 1
    )
    return jnp.concatenate(ordered + [starts, slot, lax.axis_index("seq").astype(jnp.int32)[None]])


CAP_SEQ = 44
CAP_ROW = 40


def earlier(count):
    index = jnp.arange(count, dtype=jnp.int32)
    return index[None, :] < index[:, None]


def counted(mask, axis):
    return jnp.sum(mask.astype(jnp.int32), axis)


def inverted(place, value, count):
    hit = place[None, :] == jnp.arange(count, dtype=jnp.int32)[:, None]
    return jnp.sum(jnp.where(hit, value[None, :], 0), 1)


def migration_tables(page_owner, migrate_dest, pool_size):
    rows, seqs = lax.axis_size("row"), lax.axis_size("seq")
    row, seq = lax.axis_index("row"), lax.axis_index("seq")
    limit = pool_size // 2
    cap = pool_size // (rows * seqs)
    dest = migrate_dest.reshape(rows, seqs, pool_size)[:, :, :limit]
    live = (page_owner >= 0).reshape(rows, seqs, pool_size)[:, :, :limit]
    dest = jnp.where(live, dest, -1)
    column = jnp.where(live, dest % seqs, -1)
    all_seq = jnp.arange(seqs, dtype=jnp.int32)
    in_column = counted(column[..., None, :] == all_seq[:, None], -1)
    everyone = jnp.arange(rows * seqs, dtype=jnp.int32)
    from_row = counted(dest.reshape(rows, 1, seqs * limit) == everyone[:, None], -1)
    fits = (jnp.max(in_column) <= CAP_SEQ) & (jnp.max(from_row) <= CAP_ROW)

    dest_row = lax.dynamic_index_in_dim(dest, row, 0, False)
    own = lax.dynamic_index_in_dim(dest_row, seq, 0, False)
    step = jnp.where(own >= 0, (own % seqs - seq + seqs) % seqs, -1)
    rank = counted((step[None, :] == step[:, None]) & earlier(limit), 1)
    place = jnp.where((step >= 0) & (rank < CAP_SEQ), step * CAP_SEQ + rank, -1)
    first = inverted(place, jnp.arange(limit, dtype=jnp.int32), seqs * CAP_SEQ)

    sender = (seq - all_seq + seqs) % seqs
    lists = jnp.sum(
        jnp.where((sender[:, None] == all_seq[None, :])[..., None], dest_row[None], 0), 1
    )
    lists = lists.reshape(seqs * limit)
    which = jnp.arange(seqs * limit, dtype=jnp.int32) // limit
    here = (lists >= 0) & (lists % seqs == seq)
    step = jnp.where(here, (lists // seqs - row + rows) % rows, -1)
    before = earlier(seqs * limit) & here[None, :]
    rank = counted(before & (which[None, :] == which[:, None]), 1)
    order = counted(before & (step[None, :] == step[:, None]), 1)
    place = jnp.where(here & (order < CAP_ROW), step * CAP_ROW + order, -1)
    second = inverted(place, which * CAP_SEQ + jnp.minimum(rank, CAP_SEQ - 1), rows * CAP_ROW)

    coming = counted(dest == row * seqs + seq, -1)
    ahead = (seq - all_seq + seqs) % seqs
    offset = jnp.sum(jnp.where(ahead[None, :] < ahead[:, None], coming[:, None, :], 0), -1)
    listed = (row - jnp.arange(rows, dtype=jnp.int32) + rows) % rows
    page = jnp.arange(cap, dtype=jnp.int32)
    third = (listed[:, None] * CAP_ROW + offset)[..., None] + page
    third = jnp.where(page < coming[..., None], jnp.minimum(third, rows * CAP_ROW - 1), -1)
    return fits, first, second, third.reshape(pool_size), coming.reshape(rows * seqs)


def split_kernel(table, pool_ref, *refs):
    out_refs, scratch, arrived, sems = refs[:-3], refs[-3], refs[-2], refs[-1]
    lists = len(out_refs) // 2
    length = out_refs[0].shape[0]
    copy = pltpu.make_async_copy(pool_ref.at[pl.ds(0, scratch.shape[0])], scratch, arrived)
    copy.start()
    copy.wait()
    for k in range(lists):

        def move(i, _):
            page = table[k * length + i]
            for half in range(2):
                pltpu.make_async_copy(
                    scratch.at[page, half], out_refs[half * lists + k].at[i], sems.at[half * lists + k]
                ).start()
            return 0

        lax.fori_loop(0, length, move, 0, unroll=4)
    for k, out in enumerate(out_refs):
        pltpu.make_async_copy(out, out, sems.at[k]).wait()


def split_pool(table, pool, lists):
    limit, _, page_len, width = (pool.shape[0] // 2,) + pool.shape[1:]
    length = table.shape[0] // lists
    shape = (length, page_len, width)
    return pl.pallas_call(
        split_kernel,
        out_shape=[jax.ShapeDtypeStruct(shape, pool.dtype)] * (2 * lists),
        grid_spec=pltpu.PrefetchScalarGridSpec(
            num_scalar_prefetch=1,
            grid=(1,),
            in_specs=[pl.BlockSpec(memory_space=pl.ANY)],
            out_specs=[pl.BlockSpec(memory_space=pl.ANY)] * (2 * lists),
            scratch_shapes=[
                pltpu.VMEM((limit,) + pool.shape[1:], pool.dtype),
                pltpu.SemaphoreType.DMA,
                pltpu.SemaphoreType.DMA((2 * lists,)),
            ],
        ),
        cost_estimate=pl.CostEstimate(
            flops=0, bytes_accessed=pool.size + 4 * lists * length * page_len * width, transcendentals=0
        ),
        name="split_pool",
    )(table, pool)


def resplit_kernel(count, table, *refs):
    sources, outs = refs[:count], refs[count : 2 * count]
    scratch, arrived, sems = refs[2 * count :]
    length = sources[0].shape[0]
    copies = [
        pltpu.make_async_copy(ref, scratch.at[pl.ds(k * length, length)], arrived.at[k])
        for k, ref in enumerate(sources)
    ]
    for copy in copies:
        copy.start()
    for copy in copies:
        copy.wait()
    length_out = outs[0].shape[0]
    for k, out in enumerate(outs):

        def move(i, _):
            pltpu.make_async_copy(
                scratch.at[table[k * length_out + i]], out.at[i], sems.at[k]
            ).start()
            return 0

        lax.fori_loop(0, length_out, move, 0, unroll=4)
    for k, out in enumerate(outs):
        pltpu.make_async_copy(out, out, sems.at[k]).wait()


def resplit(table, lists):
    count = len(lists)
    length, page_len, width = lists[0].shape
    shape = (table.shape[0] // count, page_len, width)
    return pl.pallas_call(
        functools.partial(resplit_kernel, count),
        out_shape=[jax.ShapeDtypeStruct(shape, lists[0].dtype)] * count,
        grid_spec=pltpu.PrefetchScalarGridSpec(
            num_scalar_prefetch=1,
            grid=(1,),
            in_specs=[pl.BlockSpec(memory_space=pl.ANY)] * count,
            out_specs=[pl.BlockSpec(memory_space=pl.ANY)] * count,
            scratch_shapes=[
                pltpu.VMEM((count * length, page_len, width), lists[0].dtype),
                pltpu.SemaphoreType.DMA((count,)),
                pltpu.SemaphoreType.DMA((count,)),
            ],
        ),
        cost_estimate=pl.CostEstimate(
            flops=0, bytes_accessed=4 * count * length * page_len * width, transcendentals=0
        ),
        name="resplit",
    )(table, *lists)


def settle_kernel(count, table, *refs):
    sources, out, scratch, zero, sems, done = refs[: 2 * count], refs[-5], refs[-4], refs[-3], refs[-2], refs[-1]
    length = sources[0].shape[0]
    copies = [
        pltpu.make_async_copy(
            ref, scratch.at[k // count, pl.ds(k % count * length, length)], sems.at[k]
        )
        for k, ref in enumerate(sources)
    ]
    for copy in copies:
        copy.start()
    zero[...] = jnp.zeros_like(zero)
    for copy in copies:
        copy.wait()

    def place_page(i, _):
        place = table[i]

        @pl.when(place >= 0)
        def _():
            for half in range(2):
                pltpu.make_async_copy(scratch.at[half, place], out.at[i, half], done).start()

        @pl.when(place < 0)
        def _():
            pltpu.make_async_copy(zero, out.at[i], done).start()

        return 0

    lax.fori_loop(0, out.shape[0], place_page, 0, unroll=4)
    pltpu.make_async_copy(out, out, done).wait()


def settle(table, keys, values):
    count = len(keys)
    length, page_len, width = keys[0].shape
    slots = table.shape[0]
    kind = keys[0].dtype
    return pl.pallas_call(
        functools.partial(settle_kernel, count),
        out_shape=jax.ShapeDtypeStruct((slots, 2, page_len, width), kind),
        grid_spec=pltpu.PrefetchScalarGridSpec(
            num_scalar_prefetch=1,
            grid=(1,),
            in_specs=[pl.BlockSpec(memory_space=pl.ANY)] * (2 * count),
            out_specs=pl.BlockSpec(memory_space=pl.ANY),
            scratch_shapes=[
                pltpu.VMEM((2, count * length, page_len, width), kind),
                pltpu.VMEM((2, page_len, width), kind),
                pltpu.SemaphoreType.DMA((2 * count,)),
                pltpu.SemaphoreType.DMA,
            ],
        ),
        cost_estimate=pl.CostEstimate(
            flops=0, bytes_accessed=8 * slots * page_len * width, transcendentals=0
        ),
        name="settle",
    )(table, *keys, *values)


def passed(lists, axis):
    return [lists[0]] + [
        lax.ppermute(part, axis, ring(axis, k)) for k, part in enumerate(lists) if k
    ]


def rotate(values, cosine, sine):
    half = values.shape[-1] // 2
    first_half = values[..., :half]
    second_half = values[..., half:]
    return jnp.concatenate(
        [first_half * cosine - second_half * sine, second_half * cosine + first_half * sine], -1
    )


def migrate_whole(kv_pool, migrate_dest, coming, device):
    pool_size = kv_pool.shape[0]
    own_dest = lax.dynamic_slice_in_dim(migrate_dest, device * pool_size, pool_size)
    send_order = jnp.argsort(own_dest, stable=True)
    moved = lax.all_to_all(
        kv_pool[send_order], ("row", "seq"), split_axis=0, concat_axis=0, tiled=True
    )
    page = jnp.arange(pool_size // coming.shape[0], dtype=jnp.int32)
    full = (page[None, :] < coming[:, None]).reshape(pool_size)
    return jnp.where(full[:, None, None, None], moved, jnp.zeros_like(moved))


def block(
    hidden_in,
    norm_gain,
    w_qkv,
    w_out,
    kv_pool,
    page_owner,
    page_fill,
    lengths,
    group_of_request,
    migrate_dest,
):
    step_count, request_count, width_here = hidden_in.shape
    ratio = HEADS // KV_HEADS
    heads_here = w_qkv.shape[1] // ((ratio + 2) * HEAD)
    first_table = migration_tables(page_owner, migrate_dest, kv_pool.shape[0])[1]
    first_table, hidden_in = lax.optimization_barrier((first_table, hidden_in))
    hidden_f = hidden_in.astype(jnp.float32)
    seqs = lax.axis_size("seq")
    lists = split_pool(first_table, kv_pool, seqs)
    key_lists = passed(lists[:seqs], "seq")
    value_lists = passed(lists[seqs:], "seq")
    row_start = lax.axis_index("row") * width_here
    gain_f = lax.dynamic_slice_in_dim(norm_gain, row_start, width_here).astype(jnp.float32)
    width = width_here * lax.axis_size("row")
    squares = jnp.sum(hidden_f * hidden_f, -1)
    partial_value = jnp.dot(
        (hidden_f * gain_f).astype(jnp.bfloat16).reshape(step_count * request_count, width_here),
        w_qkv,
        preferred_element_type=jnp.float32,
    ).astype(jnp.bfloat16)
    columns = partial_value.shape[1]
    extra = jnp.pad(jnp.stack(pieces(squares), -1), ((0, 0), (0, 0), (0, HEAD - 3)))
    partial_value = jnp.concatenate(
        [partial_value.reshape(step_count, request_count, columns), extra], 2
    )
    step_here = lax.axis_index("row")
    position = (lengths + step_here).astype(jnp.float32)
    half = HEAD // 2
    angle = position[:, None] * THETA ** (-(jnp.arange(half, dtype=jnp.float32) * 2.0 / HEAD))
    cosine, sine = lax.optimization_barrier((jnp.cos(angle), jnp.sin(angle)))
    summed = lax.dynamic_index_in_dim(partial_value, step_here, 0, False).astype(jnp.float32)
    arrived = exchanged(partial_value, "row")
    for part in arrived:
        summed = summed + part.astype(jnp.float32)
    scale = lax.rsqrt(jnp.sum(summed[:, columns : columns + 3], -1) / width + EPS)
    projected = (summed[:, :columns] * scale[:, None]).astype(jnp.bfloat16).astype(jnp.float32)
    projected = projected.reshape(request_count, heads_here * (ratio + 2), HEAD)
    rotated = rotate(projected, cosine[:, None], sine[:, None])
    is_value = jnp.arange(heads_here * (ratio + 2)) % (ratio + 2) == ratio + 1
    ready = jnp.where(is_value[None, :, None], projected, rotated).astype(jnp.bfloat16)
    ready, page_owner, migrate_dest, page_fill, group_of_request = lax.optimization_barrier(
        (ready, page_owner, migrate_dest, page_fill, group_of_request)
    )
    fits, _, second_table, third_table, coming = migration_tables(
        page_owner, migrate_dest, kv_pool.shape[0]
    )
    ready = collected(ready, "row")
    ready = ready.reshape(step_count, request_count, heads_here, ratio + 2, HEAD)
    key_lists = resplit(second_table, key_lists)
    key_lists = passed(key_lists, "row")
    queries = ready[:, :, :, :ratio]
    keys_new = ready[:, :, :, ratio]
    values_new = ready[:, :, :, ratio + 1]
    local_req = request_count // lax.axis_size("seq")
    req_start = lax.axis_index("seq") * local_req
    new_kv = jnp.stack(
        [
            keys_new.reshape(step_count, request_count, heads_here * HEAD),
            values_new.reshape(step_count, request_count, heads_here * HEAD),
        ],
        2,
    )
    new_kv_local = lax.dynamic_slice_in_dim(new_kv, req_start, local_req, 1)
    device = lax.axis_index("row") * lax.axis_size("seq") + lax.axis_index("seq")
    pool_size = kv_pool.shape[0]
    owners_here = lax.dynamic_slice_in_dim(page_owner, device * pool_size, pool_size)
    fills = lax.dynamic_slice_in_dim(page_fill, device * pool_size, pool_size)
    live_limit = pool_size // 2
    table = page_table(owners_here[:live_limit], fills[:live_limit], group_of_request)
    rows_here = step_count * ratio
    rows_first = queries[:, :, 0].transpose(1, 0, 2, 3).reshape(request_count, rows_here, HEAD)
    seq_size = lax.axis_size("seq")
    own_rows = local_req * rows_here
    both = attend(table, rows_first, kv_pool, seq_size)
    parts = passed(both, "seq")
    query_own = lax.dynamic_slice_in_dim(rows_first, req_start, local_req, 0)
    key_own = lax.dynamic_slice_in_dim(keys_new, req_start, local_req, 1)
    value_own = lax.dynamic_slice_in_dim(values_new, req_start, local_req, 1)
    own = fresh_part(
        query_own.reshape(own_rows, HEAD),
        key_own.reshape(step_count * local_req, HEAD),
        value_own.reshape(step_count * local_req, HEAD),
        step_count,
    )
    value_lists = resplit(second_table, value_lists)
    both = mix(parts)
    parts = [both] + [lax.ppermute(both, "row", ring("row", k)) for k in range(1, 4)]
    value_lists = passed(value_lists, "row")
    picked = final([own] + parts, ratio)
    partial_out = jnp.dot(picked, w_out, preferred_element_type=jnp.float32).astype(jnp.bfloat16)
    col_size = lax.axis_size("col")
    col_width = partial_out.shape[1] // col_size
    spread = partial_out.reshape(step_count * local_req, col_size, col_width).transpose(1, 0, 2)
    summed = jnp.sum(
        lax.all_to_all(spread, "col", 0, 0, tiled=True).astype(jnp.float32), 0
    )
    residual = lax.dynamic_slice_in_dim(
        lax.dynamic_slice_in_dim(hidden_f, req_start, local_req, 1),
        lax.axis_index("col") * col_width,
        col_width,
        2,
    )
    summed = summed.reshape(local_req, step_count, col_width).transpose(1, 0, 2)
    layer_out = (summed + residual).astype(jnp.bfloat16)
    moved = lax.cond(
        fits,
        lambda: settle(third_table, key_lists, value_lists),
        lambda: migrate_whole(kv_pool, migrate_dest, coming, device),
    )
    return (layer_out, new_kv_local, moved)


def solution(mesh):
    in_specs = (
        P(None, None, "row"),
        P(),
        P("row", "col"),
        P("col", "row"),
        P(("row", "seq"), None, None, "col"),
        P(),
        P(),
        P(),
        P(),
        P(),
    )
    out_specs = (
        P(None, "seq", ("row", "col")),
        P(None, "seq", None, "col"),
        P(("row", "seq"), None, None, "col"),
    )
    return jax.shard_map(block, mesh=mesh, in_specs=in_specs, out_specs=out_specs, check_vma=False)
```
